32 devices in a mesh: dp: 4 (over z), seq: 8 (over y, x, core).
Axes of the slice: x: 2, y: 2, z: 4, core: 2. Of those that a mesh axis runs over, the one named last changes fastest.
Arguments:
- hidden_in: bfloat16 [4, 1024, 1024], P('dp', 'seq'), may hold values from -6 to 6
- block_ids: int32 [4, 1024], P('dp', 'seq'), may hold values from 0 to 7, never falling along the last dimension, each value on 1 to 256 neighbouring positions
- out_grad: bfloat16 [4, 1024, 1024], P('dp', 'seq'), may hold values from -6 to 6
- norm1_gain: bfloat16 [1024], P(('dp', 'seq')), may hold values from 0.5 to 1.5
- norm1_bias: bfloat16 [1024], P(('dp', 'seq')), may hold values from -3 to 3
- q_weight: bfloat16 [1024, 1024], P(('dp', 'seq')), may hold values from -0.1875 to 0.1875
- q_bias: bfloat16 [1024], P(('dp', 'seq')), may hold values from -3 to 3
- k_weight: bfloat16 [1024, 1024], P(('dp', 'seq')), may hold values from -0.1875 to 0.1875
- v_weight: bfloat16 [1024, 1024], P(('dp', 'seq')), may hold values from -0.1875 to 0.1875
- v_bias: bfloat16 [1024], P(('dp', 'seq')), may hold values from -3 to 3
- o_weight: bfloat16 [1024, 1024], P(('dp', 'seq')), may hold values from -0.375 to 0.375
- o_bias: bfloat16 [1024], P(('dp', 'seq')), may hold values from -3 to 3
- norm2_gain: bfloat16 [1024], P(('dp', 'seq')), may hold values from 0.5 to 1.5
- norm2_bias: bfloat16 [1024], P(('dp', 'seq')), may hold values from -3 to 3
- fc1_weight: bfloat16 [1024, 4096], P(('dp', 'seq')), may hold values from -0.1875 to 0.1875
- fc1_bias: bfloat16 [4096], P(('dp', 'seq')), may hold values from -3 to 3
- fc2_weight: bfloat16 [4096, 1024], P(('dp', 'seq')), may hold values from -0.09375 to 0.09375
- fc2_bias: bfloat16 [1024], P(('dp', 'seq')), may hold values from -3 to 3
- head_limit: float32 [16], replicated, may hold values from 3 to 9
Outputs:
- hidden_out: bfloat16 [4, 1024, 1024], P('dp', 'seq')
- hidden_grad: bfloat16 [4, 1024, 1024], P('dp', 'seq')
- grad_norm1_gain: float32 [1024], P(('dp', 'seq'))
- grad_norm1_bias: float32 [1024], P(('dp', 'seq'))
- grad_q_weight: float32 [1024, 1024], P(('dp', 'seq'))
- grad_q_bias: float32 [1024], P(('dp', 'seq'))
- grad_k_weight: float32 [1024, 1024], P(('dp', 'seq'))
- grad_v_weight: float32 [1024, 1024], P(('dp', 'seq'))
- grad_v_bias: float32 [1024], P(('dp', 'seq'))
- grad_o_weight: float32 [1024, 1024], P(('dp', 'seq'))
- grad_o_bias: float32 [1024], P(('dp', 'seq'))
- grad_norm2_gain: float32 [1024], P(('dp', 'seq'))
- grad_norm2_bias: float32 [1024], P(('dp', 'seq'))
- grad_fc1_weight: float32 [1024, 4096], P(('dp', 'seq'))
- grad_fc1_bias: float32 [4096], P(('dp', 'seq'))
- grad_fc2_weight: float32 [4096, 1024], P(('dp', 'seq'))
- grad_fc2_bias: float32 [1024], P(('dp', 'seq'))
- clipped_q_weight: bfloat16 [1024, 1024], P(('dp', 'seq'))
- clipped_k_weight: bfloat16 [1024, 1024], P(('dp', 'seq'))
- head_peak: float32 [16], replicated
The draws below stay inside these ranges and needn't reach their ends.
Inputs may be any that keep to these rules, and one draw needn't show every extreme that they name: `block_ids`: along each sequence the block ids never fall; each id covers 1 to 256 consecutive positions, and some id covers exactly 256.
All inputs are finite; a program needn't handle non-finite values.
Results may differ from the reference program's by a relative error of at most 0.02.
Values may be sent and summed in bfloat16 or wider, within the bound.
No kernel may reach another device: no remote copies, remote signals or barrier semaphores. Data moves between devices by JAX's collectives and lax.ppermute only.
A program may use at most 320 MiB of HBM per device.

```python
import math
import jax
import jax.numpy as jnp
import numpy as np
from jax import lax

D = 1024
HEADS = 16
HEAD = 64
FF = 4096
BLOCK = 256
SEQ_LEN = 1024
SEQS = 4
BLOCKS = 8


def level_of(own_key, shape, pieces, low, largest):
    loudness = 1.0
    for axis_at, shards_of in pieces:
        draws = jax.random.uniform(jax.random.fold_in(jax.random.fold_in(own_key, 6), axis_at), (shards_of,), jnp.float32, low / len(pieces), largest / len(pieces))
        loudness = loudness * jnp.repeat(jnp.exp(draws), shape[axis_at] // shards_of).reshape((-1,) + (1,) * (len(shape) - 1 - axis_at))
    return loudness


def profile(number_of, total, limit, skew):
    loads = [(1 << 20) // math.isqrt(standing ** skew) + 1 for standing in range(2, number_of + 1)]
    spare, holding = total - limit - (number_of - 1), [1] * (number_of - 1)
    while spare > 0:
        movable = [i for i in range(number_of - 1) if holding[i] < limit]
        pool, remaining = sum([loads[i] for i in movable]), spare
        for i in movable:
            more = min(limit - holding[i], max(1, remaining * loads[i] // pool), spare)
            holding[i] = holding[i] + more
            spare = spare - more
    return np.array([limit] + holding)


def uneven(key, count, total, limit, lean):
    if count == 2:
        one = jax.random.randint(key, (), max(1, total - limit), min(limit, total - 1) + 1)
        return jnp.stack([one, total - one])
    tallies = jnp.asarray(profile(count, total, limit, lean), jnp.int32)
    twos = (count - 1) // 2
    source_of, receiver = tallies[1:1 + 2 * twos:2], tallies[2:2 + 2 * twos:2]
    room = jnp.minimum(source_of - 1, limit - receiver)
    shifted = jax.random.randint(jax.random.fold_in(key, 1), (twos,), 0, 1 << 20) % (room + 1)
    tallies = tallies.at[1:1 + 2 * twos:2].set(source_of - shifted).at[2:2 + 2 * twos:2].set(receiver + shifted)
    return tallies[jax.random.permutation(jax.random.fold_in(key, 2), count)]


def bell_draw(rng, extent, width, limit, split=(), kind=jnp.bfloat16):
    level = level_of(rng, extent, split, -0.22, 0.18) if split else 1.0
    values = jax.random.normal(rng, extent, jnp.float32) * width * level
    return jnp.minimum(jnp.maximum(values, -limit), limit).astype(kind)


def setup_inputs(seed: int = 0) -> dict:
    arg_keys = jax.random.split(jax.random.key(seed), 20)
    hidden_in = bell_draw(arg_keys[0], (SEQS, SEQ_LEN, D), 1.0, 6.0, ((0, 4), (1, 8)))
    block_ids = jax.vmap(lambda own: jnp.searchsorted(jnp.cumsum(uneven(own, BLOCKS, SEQ_LEN, BLOCK, 0)), jnp.arange(SEQ_LEN), side="right"))(jax.random.split(arg_keys[1], SEQS)).reshape((SEQS, SEQ_LEN)).astype(jnp.int32)
    out_grad = bell_draw(arg_keys[2], (SEQS, SEQ_LEN, D), 1.0, 6.0, ((0, 4), (1, 8)))
    norm1_gain = jnp.clip(1.0 + 0.1 * jax.random.normal(arg_keys[3], (D,), jnp.float32), 0.5, 1.5).astype(jnp.bfloat16)
    norm1_bias = bell_draw(arg_keys[4], (D,), 0.3, 3.0, ((0, 32),))
    q_weight = bell_draw(arg_keys[5], (D, D), D ** -0.5, 0.1875, ((0, 32),))
    q_bias = bell_draw(arg_keys[6], (D,), 0.3, 3.0, ((0, 32),))
    k_weight = bell_draw(arg_keys[7], (D, D), D ** -0.5, 0.1875, ((0, 32),))
    v_weight = bell_draw(arg_keys[8], (D, D), D ** -0.5, 0.1875, ((0, 32),))
    v_bias = bell_draw(arg_keys[9], (D,), 0.3, 3.0, ((0, 32),))
    o_weight = bell_draw(arg_keys[10], (D, D), (D // 4) ** -0.5, 0.375, ((0, 32),))
    o_bias = bell_draw(arg_keys[11], (D,), 0.3, 3.0, ((0, 32),))
    norm2_gain = jnp.clip(1.0 + 0.1 * jax.random.normal(arg_keys[12], (D,), jnp.float32), 0.5, 1.5).astype(jnp.bfloat16)
    norm2_bias = bell_draw(arg_keys[13], (D,), 0.3, 3.0, ((0, 32),))
    fc1_weight = bell_draw(arg_keys[14], (D, FF), D ** -0.5, 0.1875, ((0, 32),))
    fc1_bias = bell_draw(arg_keys[15], (FF,), 0.3, 3.0, ((0, 32),))
    fc2_weight = bell_draw(arg_keys[16], (FF, D), FF ** -0.5, 0.09375, ((0, 32),))
    fc2_bias = bell_draw(arg_keys[17], (D,), 0.3, 3.0, ((0, 32),))
    head_limit = jnp.clip(jax.random.uniform(arg_keys[18], (HEADS,), jnp.float32, 3.0, 9.0), 3.0, 9.0)
    return dict(hidden_in=hidden_in, block_ids=block_ids, out_grad=out_grad, norm1_gain=norm1_gain, norm1_bias=norm1_bias, q_weight=q_weight, q_bias=q_bias, k_weight=k_weight, v_weight=v_weight, v_bias=v_bias, o_weight=o_weight, o_bias=o_bias, norm2_gain=norm2_gain, norm2_bias=norm2_bias, fc1_weight=fc1_weight, fc1_bias=fc1_bias, fc2_weight=fc2_weight, fc2_bias=fc2_bias, head_limit=head_limit)


@jax.custom_vjp
def low(v):
    return lax.optimization_barrier(v.astype(jnp.bfloat16)).astype(jnp.float32)

@jax.custom_vjp
def low_back(v):
    return v

def low_keep(v):
    return (low(v), None)

def low_pass(kept, grad):
    return (grad,)

def back_keep(v):
    return (v, None)

def back_low(kept, grad):
    return (low(grad),)
low.defvjp(low_keep, low_pass)
low_back.defvjp(back_keep, back_low)
EPS = 1e-05
FLOOR = -1e+30
HIGH = lax.Precision.HIGHEST

def layer_norm(values, gain, shift):
    mean = lax.optimization_barrier(jnp.mean(values, axis=-1, keepdims=True))
    centred = values - mean
    spread = lax.optimization_barrier(jnp.mean(centred * centred, axis=-1, keepdims=True))
    return centred * lax.rsqrt(spread + EPS) * gain + shift

def matmul(left, right):
    return jnp.dot(left, right, precision=HIGH)

def slope_table():
    return 2.0 ** (-8.0 * (jnp.arange(HEADS).astype(jnp.float32) + 1.0) / HEADS)

def seq_forward(seq_tokens, seq_ids, params):
    gain_one, shift_one, w_query, b_query, w_key, w_value, b_value, w_out, b_out, gain_two, shift_two, w_up, b_up, w_down, b_down = params
    normed_one = layer_norm(seq_tokens, gain_one, shift_one)
    low_one = low(normed_one)
    queries = low_back(low(matmul(low_one, w_query) + b_query))
    keys = low_back(low(matmul(low_one, w_key)))
    values = low_back(low(matmul(low_one, w_value) + b_value))
    positions = jnp.arange(SEQ_LEN, dtype=jnp.int32)
    key_heads = keys.reshape(SEQ_LEN, HEADS, HEAD)
    value_heads = values.reshape(SEQ_LEN, HEADS, HEAD)

    def block(item):
        query_block, query_ids, query_pos = item
        raw = jnp.einsum('qhd,khd->hqk', query_block, key_heads, precision=HIGH) * 0.125
        allowed = (seq_ids[None, :] <= query_ids[:, None])[None]
        offset = (positions[None, :] - query_pos[:, None]).astype(jnp.float32)
        score = low_back(jnp.where(allowed, raw + slope_table()[:, None, None] * offset[None], FLOOR))
        probs = low(jax.nn.softmax(score, axis=-1))
        attended = jnp.einsum('hqk,khd->qhd', probs, value_heads, precision=HIGH)
        peak = lax.optimization_barrier(jnp.max(jnp.where(allowed, raw, FLOOR), axis=(1, 2)))
        return (attended, peak)
    rows = math.gcd(512, SEQ_LEN)
    blocks = SEQ_LEN // rows
    attended, peaks = lax.map(jax.checkpoint(block), (queries.reshape(blocks, rows, HEADS, HEAD), seq_ids.reshape(blocks, rows), positions.reshape(blocks, rows)))
    attention = attended.reshape(SEQ_LEN, D)
    attn_low = low_back(low(attention))
    mixed = seq_tokens + low_back(matmul(attn_low, w_out) + b_out)
    low_two = low(layer_norm(mixed, gain_two, shift_two))
    hidden_pre = low_back(matmul(low_two, w_up) + b_up)
    hidden_low = low(jax.nn.gelu(hidden_pre, approximate=True))
    result = mixed + low_back(matmul(hidden_low, w_down) + b_down)
    return (result, lax.optimization_barrier(jnp.max(peaks, axis=0)))

def reference(hidden_in, block_ids, out_grad, norm1_gain, norm1_bias, q_weight, q_bias, k_weight, v_weight, v_bias, o_weight, o_bias, norm2_gain, norm2_bias, fc1_weight, fc1_bias, fc2_weight, fc2_bias, head_limit):
    params = tuple((item.astype(jnp.float32) for item in (norm1_gain, norm1_bias, q_weight, q_bias, k_weight, v_weight, v_bias, o_weight, o_bias, norm2_gain, norm2_bias, fc1_weight, fc1_bias, fc2_weight, fc2_bias)))

    def forward(tokens_all, weights):

        def step(peak, item):
            seq_tokens, seq_ids = item
            result, seq_peak = seq_forward(seq_tokens, seq_ids, weights)
            return (jnp.maximum(peak, seq_peak), result)
        peak, results = lax.scan(step, jnp.full((HEADS,), FLOOR, jnp.float32), (tokens_all, block_ids))
        return (results, peak)
    result, backward, peak = jax.vjp(forward, hidden_in.astype(jnp.float32), params, has_aux=True)
    dinputs, dparams = backward(out_grad.astype(jnp.float32))
    factor = jnp.sqrt(head_limit / jnp.maximum(peak, head_limit))
    column = jnp.repeat(factor, HEAD)
    clipped_query = (params[2] * column[None, :]).astype(jnp.bfloat16)
    clipped_key = (params[4] * column[None, :]).astype(jnp.bfloat16)
    return (result.astype(jnp.bfloat16), dinputs.astype(jnp.bfloat16), dparams[0], dparams[1], dparams[2], dparams[3], dparams[4], dparams[5], dparams[6], dparams[7], dparams[8], dparams[9], dparams[10], dparams[11], dparams[12], dparams[13], dparams[14], clipped_query, clipped_key, peak)
```

```python
import functools

import jax
import jax.numpy as jnp
import numpy as np
from jax import lax
from jax.experimental import pallas as pl
from jax.experimental.pallas import tpu as pltpu
from jax.sharding import PartitionSpec as P

HEADS = 16
HEAD = 64


EPS = 1e-05
FLOOR = -1e30


def layer_norm(values, gain, shift):
    mean = jnp.mean(values, axis=-1, keepdims=True)
    centred = values - mean
    spread = jnp.mean(centred * centred, axis=-1, keepdims=True)
    return centred * lax.rsqrt(spread + EPS) * gain + shift


def activate(values):
    return jax.nn.gelu(values, approximate=True)


def slope_table():
    return 2.0 ** (-8.0 * (jnp.arange(HEADS, dtype=jnp.float32) + 1.0) / HEADS)


def score_block(query_heads, key_heads, query_ids, key_ids, query_pos, key_pos):
    raw = (
        jnp.einsum("sqhd,skhd->shqk", query_heads, key_heads, preferred_element_type=jnp.float32)
        * 0.125
    )
    allowed = (key_ids[:, None, :] <= query_ids[:, :, None])[:, None]
    offset = (key_pos[None, :] - query_pos[:, None]).astype(jnp.float32)
    score = jnp.where(allowed, raw + slope_table()[:, None, None] * offset[None], FLOOR)
    return (raw, allowed, score)


def project(values, weight):
    return jnp.dot(values, weight, preferred_element_type=jnp.float32)


def rows_first(left, right):
    flat_left = left.reshape(-1, left.shape[-1])
    flat_right = right.reshape(-1, right.shape[-1])
    return lax.dot_general(
        flat_left, flat_right, (((0,), (0,)), ((), ())), preferred_element_type=jnp.float32
    )


def times_transpose(values, weight):
    return lax.dot_general(
        values, weight, (((values.ndim - 1,), (1,)), ((), ())), preferred_element_type=jnp.float32
    )


def token_total(values):
    return jnp.sum(values.astype(jnp.float32), axis=(0, 1))


def unpack(gathered):
    (
        gain_one,
        shift_one,
        w_query,
        b_query,
        w_key,
        w_value,
        b_value,
        w_out,
        b_out,
        gain_two,
        shift_two,
        w_up,
        b_up,
        w_down,
        b_down,
    ) = gathered
    as_float = jnp.float32
    return (
        gain_one.astype(as_float),
        shift_one.astype(as_float),
        w_query,
        b_query.astype(as_float),
        w_key,
        w_value,
        b_value.astype(as_float),
        w_out,
        b_out.astype(as_float),
        gain_two.astype(as_float),
        shift_two.astype(as_float),
        w_up,
        b_up.astype(as_float),
        w_down,
        b_down.astype(as_float),
    )


def gather_body(
    hidden_in,
    block_ids,
    out_grad,
    norm1_gain,
    norm1_bias,
    q_weight,
    q_bias,
    k_weight,
    v_weight,
    v_bias,
    o_weight,
    o_bias,
    norm2_gain,
    norm2_bias,
    fc1_weight,
    fc1_bias,
    fc2_weight,
    fc2_bias,
    head_limit,
):
    params = (
        norm1_gain,
        norm1_bias,
        q_weight,
        q_bias,
        k_weight,
        v_weight,
        v_bias,
        o_weight,
        o_bias,
        norm2_gain,
        norm2_bias,
        fc1_weight,
        fc1_bias,
        fc2_weight,
        fc2_bias,
    )
    gathered = (
        lax.all_gather(params[0], ("dp", "seq"), axis=0, tiled=True),
        lax.all_gather(params[1], ("dp", "seq"), axis=0, tiled=True),
        lax.all_gather(params[2], ("dp", "seq"), axis=0, tiled=True),
        lax.all_gather(params[3], ("dp", "seq"), axis=0, tiled=True),
        lax.all_gather(params[4], ("dp", "seq"), axis=0, tiled=True),
        lax.all_gather(params[5], ("dp", "seq"), axis=0, tiled=True),
        lax.all_gather(params[6], ("dp", "seq"), axis=0, tiled=True),
        lax.all_gather(params[7], ("dp", "seq"), axis=0, tiled=True),
        lax.all_gather(params[8], ("dp", "seq"), axis=0, tiled=True),
        lax.all_gather(params[9], ("dp", "seq"), axis=0, tiled=True),
        lax.all_gather(params[10], ("dp", "seq"), axis=0, tiled=True),
        lax.all_gather(params[11], ("dp", "seq"), axis=0, tiled=True),
        lax.all_gather(params[12], ("dp", "seq"), axis=0, tiled=True),
        lax.all_gather(params[13], ("dp", "seq"), axis=0, tiled=True),
        lax.all_gather(params[14], ("dp", "seq"), axis=0, tiled=True),
    )
    (
        gain_one,
        shift_one,
        w_query,
        b_query,
        w_key,
        w_value,
        b_value,
        w_out,
        b_out,
        gain_two,
        shift_two,
        w_up,
        b_up,
        w_down,
        b_down,
    ) = unpack(gathered)
    seqs_dev, tokens, width = hidden_in.shape
    inputs = hidden_in.astype(jnp.float32)
    normed_one = layer_norm(inputs, gain_one, shift_one)
    low_one = normed_one.astype(jnp.bfloat16)
    queries = (project(low_one, w_query) + b_query).astype(jnp.bfloat16)
    keys = project(low_one, w_key).astype(jnp.bfloat16)
    values = (project(low_one, w_value) + b_value).astype(jnp.bfloat16)
    all_ids = lax.all_gather(block_ids, "seq", axis=1, tiled=True)
    query_pos = lax.axis_index("seq") * tokens + jnp.arange(tokens, dtype=jnp.int32)
    query_heads = queries.reshape(seqs_dev, tokens, HEADS, HEAD)
    key_heads_local = keys.reshape(seqs_dev, tokens, HEADS, HEAD)
    value_heads_local = values.reshape(seqs_dev, tokens, HEADS, HEAD)
    run_max = jnp.full((seqs_dev, HEADS, tokens), FLOOR, jnp.float32)
    peak = jnp.full((HEADS,), FLOOR, jnp.float32)
    key_part = lax.all_gather(keys, "seq", axis=1, tiled=True)
    value_part = lax.all_gather(values, "seq", axis=1, tiled=True)
    count = key_part.shape[1]
    key_heads = key_part.reshape(seqs_dev, count, HEADS, HEAD)
    value_heads = value_part.reshape(seqs_dev, count, HEADS, HEAD)
    key_ids = all_ids
    key_pos = jnp.arange(count, dtype=jnp.int32)
    raw, allowed, score = score_block(
        query_heads, key_heads, block_ids, key_ids, query_pos, key_pos
    )
    new_max = jnp.maximum(run_max, jnp.max(score, axis=-1))
    probs = jnp.exp(score - new_max[..., None])
    run_total = jnp.sum(probs, axis=-1)
    weighted = jnp.einsum(
        "shqk,skhd->sqhd",
        probs.astype(jnp.bfloat16),
        value_heads,
        preferred_element_type=jnp.float32,
    )
    peak = jnp.maximum(peak, jnp.max(jnp.where(allowed, raw, FLOOR), axis=(0, 2, 3)))
    run_max, run_total, weighted, peak = (new_max, run_total, weighted, peak)
    head_peak = lax.pmax(peak, ("dp", "seq"))
    log_total = run_max + jnp.log(run_total)
    attention = (weighted / jnp.transpose(run_total, (0, 2, 1))[..., None]).reshape(
        seqs_dev, tokens, width
    )
    attn_low = attention.astype(jnp.bfloat16)
    mixed = inputs + project(attn_low, w_out) + b_out
    normed_two = layer_norm(mixed, gain_two, shift_two)
    low_two = normed_two.astype(jnp.bfloat16)
    hidden_pre = project(low_two, w_up) + b_up
    hidden_low = activate(hidden_pre).astype(jnp.bfloat16)
    hidden_out = (mixed + project(hidden_low, w_down) + b_down).astype(jnp.bfloat16)
    regathered = (
        lax.all_gather(params[0], ("dp", "seq"), axis=0, tiled=True),
        lax.all_gather(params[1], ("dp", "seq"), axis=0, tiled=True),
        lax.all_gather(params[2], ("dp", "seq"), axis=0, tiled=True),
        lax.all_gather(params[3], ("dp", "seq"), axis=0, tiled=True),
        lax.all_gather(params[4], ("dp", "seq"), axis=0, tiled=True),
        lax.all_gather(params[5], ("dp", "seq"), axis=0, tiled=True),
        lax.all_gather(params[6], ("dp", "seq"), axis=0, tiled=True),
        lax.all_gather(params[7], ("dp", "seq"), axis=0, tiled=True),
        lax.all_gather(params[8], ("dp", "seq"), axis=0, tiled=True),
        lax.all_gather(params[9], ("dp", "seq"), axis=0, tiled=True),
        lax.all_gather(params[10], ("dp", "seq"), axis=0, tiled=True),
        lax.all_gather(params[11], ("dp", "seq"), axis=0, tiled=True),
        lax.all_gather(params[12], ("dp", "seq"), axis=0, tiled=True),
        lax.all_gather(params[13], ("dp", "seq"), axis=0, tiled=True),
        lax.all_gather(params[14], ("dp", "seq"), axis=0, tiled=True),
    )
    (
        gain_one,
        shift_one,
        w_query,
        b_query,
        w_key,
        w_value,
        b_value,
        w_out,
        b_out,
        gain_two,
        shift_two,
        w_up,
        b_up,
        w_down,
        b_down,
    ) = unpack(regathered)
    dout = out_grad.astype(jnp.float32)
    grad_b_down = jnp.sum(dout, axis=(0, 1))
    grad_w_down = rows_first(hidden_low, out_grad)
    dhidden = times_transpose(out_grad, w_down)
    unused_gelu, gelu_back = jax.vjp(activate, hidden_pre)
    dpre_low = gelu_back(dhidden)[0].astype(jnp.bfloat16)
    grad_b_up = token_total(dpre_low)
    grad_w_up = rows_first(low_two, dpre_low)
    dnormed_two = times_transpose(dpre_low, w_up)
    unused_two, norm_back_two = jax.vjp(layer_norm, mixed, gain_two, shift_two)
    dmixed_part, grad_gain_two, grad_shift_two = norm_back_two(dnormed_two)
    dmixed = dout + dmixed_part
    dbranch = dmixed.astype(jnp.bfloat16)
    grad_b_out = token_total(dbranch)
    grad_w_out = rows_first(attn_low, dbranch)
    later_terms = (
        grad_w_out,
        grad_b_out,
        grad_gain_two,
        grad_shift_two,
        grad_w_up,
        grad_b_up,
        grad_w_down,
        grad_b_down,
    )
    dattention = times_transpose(dbranch, w_out).astype(jnp.bfloat16)
    delta = jnp.transpose(
        jnp.sum(
            (dattention.astype(jnp.float32) * attention).reshape(seqs_dev, tokens, HEADS, HEAD),
            axis=-1,
        ),
        (0, 2, 1),
    )
    all_log, all_delta = (
        lax.all_gather(log_total, "seq", axis=2, tiled=True),
        lax.all_gather(delta, "seq", axis=2, tiled=True),
    )
    dout_heads = dattention.reshape(seqs_dev, tokens, HEADS, HEAD)
    key_part = lax.all_gather(keys, "seq", axis=1, tiled=True)
    value_part = lax.all_gather(values, "seq", axis=1, tiled=True)
    count = key_part.shape[1]
    key_heads = key_part.reshape(seqs_dev, count, HEADS, HEAD)
    value_heads = value_part.reshape(seqs_dev, count, HEADS, HEAD)
    key_ids = all_ids
    key_pos = jnp.arange(count, dtype=jnp.int32)
    raw, allowed, score = score_block(
        query_heads, key_heads, block_ids, key_ids, query_pos, key_pos
    )
    probs = jnp.exp(score - log_total[..., None])
    dprobs = jnp.einsum(
        "sqhd,skhd->shqk", dout_heads, value_heads, preferred_element_type=jnp.float32
    )
    dscores = (probs * (dprobs - delta[..., None])).astype(jnp.bfloat16)
    dquery = 0.125 * jnp.einsum(
        "shqk,skhd->sqhd", dscores, key_heads, preferred_element_type=jnp.float32
    )
    query_part = lax.all_gather(queries, "seq", axis=1, tiled=True)
    dout_part = lax.all_gather(dattention, "seq", axis=1, tiled=True)
    count = query_part.shape[1]
    part_queries = query_part.reshape(seqs_dev, count, HEADS, HEAD)
    part_douts = dout_part.reshape(seqs_dev, count, HEADS, HEAD)
    part_pos = jnp.arange(count, dtype=jnp.int32)
    raw, allowed, score = score_block(
        part_queries, key_heads_local, all_ids, block_ids, part_pos, query_pos
    )
    probs = jnp.exp(score - all_log[..., None])
    value_total = jnp.einsum(
        "shqk,sqhd->skhd",
        probs.astype(jnp.bfloat16),
        part_douts,
        preferred_element_type=jnp.float32,
    )
    dprobs = jnp.einsum(
        "sqhd,skhd->shqk", part_douts, value_heads_local, preferred_element_type=jnp.float32
    )
    dscores = (probs * (dprobs - all_delta[..., None])).astype(jnp.bfloat16)
    key_total = 0.125 * jnp.einsum(
        "shqk,sqhd->skhd", dscores, part_queries, preferred_element_type=jnp.float32
    )
    dquery_low = dquery.reshape(seqs_dev, tokens, width).astype(jnp.bfloat16)
    dkey_low = key_total.reshape(seqs_dev, tokens, width).astype(jnp.bfloat16)
    dvalue_low = value_total.reshape(seqs_dev, tokens, width).astype(jnp.bfloat16)
    grad_b_query = token_total(dquery_low)
    grad_b_value = token_total(dvalue_low)
    grad_w_query = rows_first(low_one, dquery_low)
    grad_w_key = rows_first(low_one, dkey_low)
    grad_w_value = rows_first(low_one, dvalue_low)
    dnormed_one = (
        times_transpose(dquery_low, w_query)
        + times_transpose(dkey_low, w_key)
        + times_transpose(dvalue_low, w_value)
    )
    unused_one, norm_back_one = jax.vjp(layer_norm, inputs, gain_one, shift_one)
    dinputs_part, grad_gain_one, grad_shift_one = norm_back_one(dnormed_one)
    hidden_grad = (dmixed + dinputs_part).astype(jnp.bfloat16)
    earlier_terms = (
        grad_gain_one,
        grad_shift_one,
        grad_w_query,
        grad_b_query,
        grad_w_key,
        grad_w_value,
        grad_b_value,
    )
    shards = tuple(
        lax.psum_scatter(
            earlier_terms + later_terms, ("dp", "seq"), scatter_dimension=0, tiled=True
        )
    )
    factor = jnp.sqrt(head_limit / jnp.maximum(head_peak, head_limit))
    column = jnp.repeat(factor, HEAD)
    clipped_query = (q_weight.astype(jnp.float32) * column[None, :]).astype(jnp.bfloat16)
    clipped_key = (k_weight.astype(jnp.float32) * column[None, :]).astype(jnp.bfloat16)
    return (hidden_out, hidden_grad) + shards + (clipped_query, clipped_key, head_peak)


BF16 = jnp.bfloat16
F32 = jnp.float32


def lanes_dot(left, right, left_dim, right_dim):
    return lax.dot_general(
        left, right, (((left_dim,), (right_dim,)), ((), ())), preferred_element_type=F32
    )


def half_lanes(values, which):
    lane = lax.broadcasted_iota(jnp.int32, values.shape, 1)
    keep = lane < HEAD if which == 0 else lane >= HEAD
    return jnp.where(keep, values, jnp.zeros_like(values))


def attend_kernel(slopes, q_ref, k_ref, v_ref, k2_ref, v2_ref, key_ref, query_ref, out_ref, stat_ref):
    pair = pl.program_id(0)
    allowed = key_ref[:, 1:2] <= query_ref[1:2, :]
    offset = key_ref[:, 0:1] - query_ref[0:1, :]
    keys = jnp.concatenate([k_ref[...], k2_ref[...]], axis=0)
    values = jnp.concatenate([v_ref[...], v2_ref[...]], axis=0)
    queries = q_ref[...] * jnp.asarray(0.125, BF16)
    mixes, logs, peaks = [], [], []
    for a in range(2):
        raw = lanes_dot(keys, half_lanes(queries, a), 1, 1)
        score = jnp.where(allowed, raw + slopes[2 * pair + a] * offset, FLOOR)
        top = jnp.max(score, axis=0, keepdims=True)
        probs = jnp.exp(score - top)
        total = jnp.sum(probs, axis=0, keepdims=True)
        mix = lanes_dot(values, probs.astype(BF16), 0, 0)
        mixes.append(mix[a * HEAD : (a + 1) * HEAD] / total)
        logs.append(top + jnp.log(total))
        peaks.append(jnp.max(jnp.where(allowed, raw, FLOOR), axis=0, keepdims=True))
    out_ref[...] = jnp.concatenate(mixes, axis=0).T.astype(BF16)
    stat_ref[...] = jnp.concatenate(logs + peaks + logs + peaks, axis=0)


def attend_back_kernel(
    slopes, q_ref, do_ref, k_ref, v_ref, k2_ref, v2_ref, key_ref, query_ref, stat_ref,
    dq_ref, dk_ref, dv_ref,
):
    pair = pl.program_id(0)
    step = pl.program_id(1)
    allowed = key_ref[:, 1:2] <= query_ref[1:2, :]
    offset = key_ref[:, 0:1] - query_ref[0:1, :]
    keys = jnp.concatenate([k_ref[...], k2_ref[...]], axis=0)
    values = jnp.concatenate([v_ref[...], v2_ref[...]], axis=0)
    queries = q_ref[...] * jnp.asarray(0.125, BF16)
    douts = do_ref[...]
    dqs, dk, dv = [], None, None
    for a in range(2):
        query = half_lanes(queries, a)
        dout = half_lanes(douts, a)
        raw = lanes_dot(keys, query, 1, 1)
        score = jnp.where(allowed, raw + slopes[2 * pair + a] * offset, FLOOR)
        probs = jnp.exp(score - stat_ref[a : a + 1, :])
        dprobs = lanes_dot(values, dout, 1, 1)
        delta = jnp.sum(probs * dprobs, axis=0, keepdims=True)
        dscores = (probs * (dprobs - delta)).astype(BF16)
        dv_part = lanes_dot(probs.astype(BF16), dout, 1, 0)
        dk_part = lanes_dot(dscores, query, 1, 0)
        dv = dv_part if dv is None else dv + dv_part
        dk = dk_part if dk is None else dk + dk_part
        dqs.append(lanes_dot(keys, dscores, 0, 0)[a * HEAD : (a + 1) * HEAD] * 0.125)
    dq_ref[...] = jnp.concatenate(dqs, axis=0).T.astype(BF16)

    @pl.when(step == 0)
    def _():
        dk_ref[...] = dk
        dv_ref[...] = dv

    @pl.when(step > 0)
    def _():
        dk_ref[...] += dk
        dv_ref[...] += dv


def query_chunk(count):
    return 256 if count % 256 == 0 else count


def attention_specs(count, chunk, pairs):
    lanes = 2 * HEAD
    own = lambda first: pl.BlockSpec((count, lanes), lambda i, j: (0, first + i))
    return dict(
        slopes=pl.BlockSpec(memory_space=pltpu.SMEM),
        query=pl.BlockSpec((chunk, lanes), lambda i, j: (j, i)),
        key=own(pairs),
        value=own(2 * pairs),
        key_two=own(0),
        value_two=own(pairs),
        key_rows=pl.BlockSpec((2 * count, 2), lambda i, j: (0, 0)),
        query_rows=pl.BlockSpec((2, chunk), lambda i, j: (0, j)),
        stats=pl.BlockSpec((8, chunk), lambda i, j: (i, j)),
        whole=pl.BlockSpec((2 * count, lanes), lambda i, j: (0, i)),
    )


def attend(slopes, qkv, kv_two, key_rows, query_rows):
    count, pairs = qkv.shape[0], slopes.shape[0] // 2
    chunk = query_chunk(count)
    specs = attention_specs(count, chunk, pairs)
    work = 2 * count * count * 2 * HEAD * 2 * pairs
    return pl.pallas_call(
        attend_kernel,
        grid=(pairs, count // chunk),
        in_specs=[specs[n] for n in (
            "slopes", "query", "key", "value", "key_two", "value_two", "key_rows", "query_rows")],
        out_specs=[specs["query"], specs["stats"]],
        out_shape=[
            jax.ShapeDtypeStruct((count, pairs * 2 * HEAD), BF16),
            jax.ShapeDtypeStruct((pairs * 8, count), F32),
        ],
        cost_estimate=pl.CostEstimate(
            flops=4 * work, bytes_accessed=8 * count * pairs * 2 * HEAD,
            transcendentals=4 * pairs * count * count,
        ),
        compiler_params=pltpu.CompilerParams(vmem_limit_bytes=48 * 1024 * 1024),
        name="attend",
    )(slopes, qkv, qkv, qkv, kv_two, kv_two, key_rows, query_rows)


def attend_back(slopes, qkv, douts, kv_two, key_rows, query_rows, stats):
    count, pairs = qkv.shape[0], slopes.shape[0] // 2
    chunk = query_chunk(count)
    specs = attention_specs(count, chunk, pairs)
    work = 2 * count * count * 2 * HEAD * 2 * pairs
    return pl.pallas_call(
        attend_back_kernel,
        grid=(pairs, count // chunk),
        in_specs=[specs[n] for n in (
            "slopes", "query", "query", "key", "value", "key_two", "value_two", "key_rows",
            "query_rows", "stats")],
        out_specs=[specs["query"], specs["whole"], specs["whole"]],
        out_shape=[
            jax.ShapeDtypeStruct((count, pairs * 2 * HEAD), BF16),
            jax.ShapeDtypeStruct((2 * count, pairs * 2 * HEAD), F32),
            jax.ShapeDtypeStruct((2 * count, pairs * 2 * HEAD), F32),
        ],
        cost_estimate=pl.CostEstimate(
            flops=10 * work, bytes_accessed=24 * count * pairs * 2 * HEAD,
            transcendentals=4 * pairs * count * count,
        ),
        compiler_params=pltpu.CompilerParams(vmem_limit_bytes=48 * 1024 * 1024),
        name="attend_back",
    )(slopes, qkv, douts, qkv, qkv, kv_two, kv_two, key_rows, query_rows, stats)


def flips(size, step):
    return [(i, i ^ step) for i in range(size)]


def pick(values, index, axis=0):
    return lax.dynamic_index_in_dim(values, index, axis, keepdims=False)


def in_order(parts, me):
    stacked = jnp.stack(parts)
    return jnp.stack([pick(stacked, me ^ j) for j in range(len(parts))])


def split_body(planes, seq_size, *args):
    (
        hidden_in,
        block_ids,
        out_grad,
        norm1_gain,
        norm1_bias,
        q_weight,
        q_bias,
        k_weight,
        v_weight,
        v_bias,
        o_weight,
        o_bias,
        norm2_gain,
        norm2_bias,
        fc1_weight,
        fc1_bias,
        fc2_weight,
        fc2_bias,
        head_limit,
    ) = args
    chips = seq_size // 2
    plane = lax.axis_index("dp")
    spot = lax.axis_index("seq")
    chip, core = spot // 2, spot % 2
    tokens, width = hidden_in.shape[1:]
    rows = q_weight.shape[0]
    units = fc2_weight.shape[0]
    count = chips * tokens

    def to_chip(values, r):
        return lax.ppermute(values, "seq", flips(seq_size, 2 * r))

    def to_core(values):
        return lax.ppermute(values, "seq", flips(seq_size, 1))

    def to_plane(values, j):
        return lax.ppermute(values, "dp", flips(planes, j))

    def spread(values):
        return [values] + [to_chip(values, r) for r in range(1, chips)]

    def fold(partial):
        blocks = partial.reshape(chips, tokens, width)
        total = blocks[0]
        for r in range(1, chips):
            total = total + to_chip(blocks[r].astype(BF16), r).astype(F32)
        return total

    def deal(parts, kind=BF16):
        return [pick(parts, chip)] + [
            to_chip(pick(parts, chip ^ r).astype(kind), r) for r in range(1, chips)
        ]

    def from_planes(values):
        return in_order([values] + [to_plane(values, j) for j in range(1, planes)], plane)

    def plane_total(parts, kind=BF16):
        total = pick(parts, plane)
        for j in range(1, planes):
            total = total + to_plane(pick(parts, plane ^ j).astype(kind), j).astype(F32)
        return total

    def weave(mine, other, axis):
        return jnp.where(
            core == 0, jnp.stack([mine, other], axis=axis), jnp.stack([other, mine], axis=axis)
        )

    def core_total(parts, axis, kind=BF16):
        return pick(parts, core, axis) + to_core(
            pick(parts, 1 - core, axis).astype(kind)
        ).astype(F32)

    def column_parts(weight):
        share = weight.reshape(weight.shape[0], planes, chips, -1)
        return jnp.transpose(share, (2, 0, 1, 3)).reshape(chips, weight.shape[0], -1)

    small = jnp.concatenate(
        [norm1_gain, norm1_bias, q_bias, v_bias, o_bias, norm2_gain, norm2_bias, fc2_bias, fc1_bias]
        + [block_ids.reshape(-1).astype(BF16)]
    )
    hidden = jnp.concatenate(spread(hidden_in[0]), axis=0)
    table = lax.all_gather(small, ("dp", "seq"), axis=0, tiled=False).astype(F32)
    by_chip = table.reshape(planes, chips, 2, -1)
    mine_by_chip = pick(by_chip, chip, 1)

    def vector(i):
        return by_chip[..., i * rows : (i + 1) * rows].reshape(width)

    def chip_vector(i):
        return mine_by_chip[..., i * rows : (i + 1) * rows].reshape(-1)

    gain_one, shift_one, b_out, gain_two, shift_two, b_down = (
        vector(i) for i in (0, 1, 4, 5, 6, 7)
    )
    b_query, b_value = chip_vector(2), chip_vector(3)
    b_up = mine_by_chip[..., 8 * rows : 8 * rows + units].reshape(-1)
    ids = pick(table.reshape(planes, seq_size, -1), plane)[:, 8 * rows + units :]
    near = [spot ^ (2 * r) for r in range(chips)]
    order = near + [at ^ 1 for at in near]
    key_ids = jnp.concatenate([pick(ids, at) for at in order])
    lane = jnp.arange(tokens, dtype=jnp.int32)
    key_pos = jnp.concatenate([(at * tokens + lane).astype(F32) for at in order])
    key_rows = jnp.stack([key_pos, key_ids], axis=1)
    query_rows = jnp.stack([key_pos[:count], key_ids[:count]], axis=0)
    slope_host = 2.0 ** (-8.0 * (np.arange(HEADS, dtype=np.float64) + 1.0) / HEADS)
    slopes = pick(jnp.asarray(slope_host.reshape(planes, chips), F32), chip, 1)

    qkv_parts = jnp.concatenate([column_parts(w) for w in (q_weight, k_weight, v_weight)], axis=2)
    qkv_mine = from_planes(in_order(deal(qkv_parts), chip))
    w_qkv = weave(qkv_mine, to_core(qkv_mine), 2).reshape(width, -1)
    out_mine = jnp.stack(spread(from_planes(o_weight)))
    w_out = weave(out_mine, to_core(out_mine), 2).reshape(width, width)
    up_mine = from_planes(in_order(deal(column_parts(fc1_weight)), chip))
    w_up = weave(up_mine, to_core(up_mine), 2).reshape(width, -1)
    down_mine = from_planes(fc2_weight)
    w_down = weave(down_mine, to_core(down_mine), 1).reshape(-1, width)
    share = w_qkv.shape[1] // 3
    douts = jnp.concatenate(spread(out_grad[0]), axis=0)

    inputs = hidden.astype(F32)
    low_one = layer_norm(inputs, gain_one, shift_one).astype(BF16)
    qkv_bias = jnp.concatenate([b_query, jnp.zeros_like(b_query), b_value])
    qkv = (project(low_one, w_qkv) + qkv_bias).astype(BF16)
    kv_two = to_core(qkv[:, share:])
    attn_low, stats = attend(slopes, qkv, kv_two, key_rows, query_rows)
    attn_all = [part.reshape(chips, tokens, -1) for part in spread(attn_low)]
    attn_all = jnp.concatenate(
        [jnp.stack([part[j ^ r] for j in range(chips)]) for r, part in enumerate(attn_all)], axis=2
    ).reshape(count, width)
    mixed = inputs + project(attn_all, w_out) + b_out
    low_two = layer_norm(mixed, gain_two, shift_two).astype(BF16)
    hidden_pre = project(low_two, w_up) + b_up
    hidden_low, gelu_back = jax.vjp(activate, hidden_pre)
    hidden_low = hidden_low.astype(BF16)

    dhidden = times_transpose(douts, w_down)
    dpre_low = gelu_back(dhidden)[0].astype(BF16)
    dnormed_two = fold(times_transpose(dpre_low, w_up))
    mixed_own = mixed[:tokens]
    unused_two, norm_back_two = jax.vjp(layer_norm, mixed_own, gain_two, shift_two)
    dmixed_part, grad_gain_two, grad_shift_two = norm_back_two(dnormed_two)
    dmixed = out_grad[0].astype(F32) + dmixed_part
    dbranch = jnp.concatenate(spread(dmixed.astype(BF16)), axis=0)
    hidden_out = (mixed_own + fold(project(hidden_low, w_down)) + b_down).astype(BF16)
    grad_w_down = plane_total(
        core_total(rows_first(hidden_low, douts).reshape(planes, 2, units, width), 1)
    )

    def column_grad(partial, pieces):
        cols = partial.shape[1]
        own = core_total(partial.reshape(planes, chips, 2, rows, cols), 2)
        parts = in_order([p.astype(F32) for p in deal(plane_total(own))], chip)
        parts = parts.reshape(chips, rows, pieces, planes, -1)
        return jnp.transpose(parts, (2, 1, 3, 0, 4)).reshape(pieces, rows, -1)

    grad_w_up = column_grad(rows_first(low_two, dpre_low), 1)[0]

    dattention = times_transpose(dbranch, w_out[:share]).astype(BF16)
    grad_w_out = plane_total(
        core_total(rows_first(attn_low, dbranch).reshape(planes, 2, rows, width), 1)
    )
    dquery, dkey, dvalue = attend_back(
        slopes, qkv, dattention, kv_two, key_rows, query_rows, stats
    )
    dkv_two = to_core(jnp.concatenate([dkey[count:], dvalue[count:]], axis=1).astype(BF16))
    dkv = (
        jnp.concatenate([dkey[:count], dvalue[:count]], axis=1) + dkv_two.astype(F32)
    ).astype(BF16)
    dqkv = jnp.concatenate([dquery, dkv], axis=1)
    dnormed_one = fold(times_transpose(dqkv, w_qkv))
    unused_one, norm_back_one = jax.vjp(layer_norm, inputs[:tokens], gain_one, shift_one)
    dinputs_part, grad_gain_one, grad_shift_one = norm_back_one(dnormed_one)
    hidden_grad = (dmixed + dinputs_part).astype(BF16)
    grad_w_query, grad_w_key, grad_w_value = column_grad(rows_first(low_one, dqkv), 3)

    norms = jnp.stack([grad_gain_one, grad_shift_one, grad_gain_two, grad_shift_two])
    norms = norms.reshape(4, planes, chips, 2, rows)
    norms = sum(deal(jnp.transpose(norms, (2, 1, 3, 0, 4)), F32)).reshape(planes, 2, 4 * rows)
    by_feature = jnp.stack(
        [jnp.sum(dbranch.astype(F32), axis=0), jnp.sum(douts.astype(F32), axis=0)]
    ).reshape(2, planes, chips, 2, rows)
    by_feature = jnp.transpose(pick(by_feature, chip, 2), (1, 2, 0, 3)).reshape(planes, 2, 2 * rows)
    dqkv_total = jnp.sum(dqkv.astype(F32), axis=0).reshape(3, planes, 2, rows)
    dpre_total = jnp.sum(dpre_low.astype(F32), axis=0).reshape(planes, 2, units)
    sums = jnp.concatenate([norms, dqkv_total[0], dqkv_total[2], by_feature, dpre_total], axis=2)
    sums = plane_total(core_total(sums, 1, F32), F32)
    (
        g_gain_one, g_shift_one, g_gain_two, g_shift_two, g_b_query, g_b_value, g_b_out, g_b_down,
    ) = (sums[i * rows : (i + 1) * rows] for i in range(8))
    g_b_up = sums[8 * rows :]

    peaks = jnp.max(stats.reshape(-1, 8, count)[:, 2:4], axis=2).reshape(planes, 1)
    head_peak = jnp.where(jnp.arange(chips)[None, :] == chip, peaks, FLOOR).reshape(HEADS)
    step = 1
    while step < seq_size:
        head_peak = jnp.maximum(head_peak, lax.ppermute(head_peak, "seq", flips(seq_size, step)))
        step *= 2
    step = 1
    while step < planes:
        head_peak = jnp.maximum(head_peak, to_plane(head_peak, step))
        step *= 2
    factor = jnp.sqrt(head_limit / jnp.maximum(head_peak, head_limit))
    column = jnp.repeat(factor, HEAD)
    clipped_query = (q_weight.astype(F32) * column[None, :]).astype(BF16)
    clipped_key = (k_weight.astype(F32) * column[None, :]).astype(BF16)
    return (
        hidden_out[None],
        hidden_grad[None],
        g_gain_one,
        g_shift_one,
        grad_w_query,
        g_b_query,
        grad_w_key,
        grad_w_value,
        g_b_value,
        grad_w_out,
        g_b_out,
        g_gain_two,
        g_shift_two,
        grad_w_up,
        g_b_up,
        grad_w_down,
        g_b_down,
        clipped_query,
        clipped_key,
        head_peak,
    )


def power_of_two(number):
    return number & (number - 1) == 0


def body(planes, seq_size, *args):
    seqs_dev, tokens, width = args[0].shape
    chips = seq_size // 2
    heads_split = planes * chips * HEAD == width and planes % 2 == 0
    sizes_fit = seq_size % 2 == 0 and power_of_two(chips) and power_of_two(planes)
    if heads_split and sizes_fit and seqs_dev == 1:
        return split_body(planes, seq_size, *args)
    return gather_body(*args)


def solution(mesh):
    return jax.shard_map(
        functools.partial(body, mesh.shape["dp"], mesh.shape["seq"]),
        mesh=mesh,
        in_specs=(
            P("dp", "seq", None),
            P("dp", "seq"),
            P("dp", "seq", None),
            P(("dp", "seq")),
            P(("dp", "seq")),
            P(("dp", "seq"), None),
            P(("dp", "seq")),
            P(("dp", "seq"), None),
            P(("dp", "seq"), None),
            P(("dp", "seq")),
            P(("dp", "seq"), None),
            P(("dp", "seq")),
            P(("dp", "seq")),
            P(("dp", "seq")),
            P(("dp", "seq"), None),
            P(("dp", "seq")),
            P(("dp", "seq"), None),
            P(("dp", "seq")),
            P(),
        ),
        out_specs=(
            P("dp", "seq", None),
            P("dp", "seq", None),
            P(("dp", "seq")),
            P(("dp", "seq")),
            P(("dp", "seq"), None),
            P(("dp", "seq")),
            P(("dp", "seq"), None),
            P(("dp", "seq"), None),
            P(("dp", "seq")),
            P(("dp", "seq"), None),
            P(("dp", "seq")),
            P(("dp", "seq")),
            P(("dp", "seq")),
            P(("dp", "seq"), None),
            P(("dp", "seq")),
            P(("dp", "seq"), None),
            P(("dp", "seq")),
            P(("dp", "seq"), None),
            P(("dp", "seq"), None),
            P(),
        ),
        check_vma=False,
    )
```

```python
import functools

import jax
import jax.numpy as jnp
import numpy as np
from jax import lax
from jax.experimental import pallas as pl
from jax.experimental.pallas import tpu as pltpu
from jax.sharding import PartitionSpec as P


HEADS = 16
HEAD = 64


EPS = 1e-05
FLOOR = -1e30


def layer_norm(values, gain, shift):
    mean = jnp.mean(values, axis=-1, keepdims=True)
    centred = values - mean
    spread = jnp.mean(centred * centred, axis=-1, keepdims=True)
    return centred * lax.rsqrt(spread + EPS) * gain + shift


def activate(values):
    return jax.nn.gelu(values, approximate=True)


def slope_table():
    return 2.0 ** (-8.0 * (jnp.arange(HEADS, dtype=jnp.float32) + 1.0) / HEADS)


def score_block(query_heads, key_heads, query_ids, key_ids, query_pos, key_pos):
    raw = (
        jnp.einsum("sqhd,skhd->shqk", query_heads, key_heads, preferred_element_type=jnp.float32)
        * 0.125
    )
    allowed = (key_ids[:, None, :] <= query_ids[:, :, None])[:, None]
    offset = (key_pos[None, :] - query_pos[:, None]).astype(jnp.float32)
    score = jnp.where(allowed, raw + slope_table()[:, None, None] * offset[None], FLOOR)
    return (raw, allowed, score)


def project(values, weight):
    return jnp.dot(values, weight, preferred_element_type=jnp.float32)


def rows_first(left, right):
    flat_left = left.reshape(-1, left.shape[-1])
    flat_right = right.reshape(-1, right.shape[-1])
    return lax.dot_general(
        flat_left, flat_right, (((0,), (0,)), ((), ())), preferred_element_type=jnp.float32
    )


def times_transpose(values, weight):
    return lax.dot_general(
        values, weight, (((values.ndim - 1,), (1,)), ((), ())), preferred_element_type=jnp.float32
    )


def token_total(values):
    return jnp.sum(values.astype(jnp.float32), axis=(0, 1))


def unpack(gathered):
    (
        gain_one,
        shift_one,
        w_query,
        b_query,
        w_key,
        w_value,
        b_value,
        w_out,
        b_out,
        gain_two,
        shift_two,
        w_up,
        b_up,
        w_down,
        b_down,
    ) = gathered
    as_float = jnp.float32
    return (
        gain_one.astype(as_float),
        shift_one.astype(as_float),
        w_query,
        b_query.astype(as_float),
        w_key,
        w_value,
        b_value.astype(as_float),
        w_out,
        b_out.astype(as_float),
        gain_two.astype(as_float),
        shift_two.astype(as_float),
        w_up,
        b_up.astype(as_float),
        w_down,
        b_down.astype(as_float),
    )


def gather_body(
    hidden_in,
    block_ids,
    out_grad,
    norm1_gain,
    norm1_bias,
    q_weight,
    q_bias,
    k_weight,
    v_weight,
    v_bias,
    o_weight,
    o_bias,
    norm2_gain,
    norm2_bias,
    fc1_weight,
    fc1_bias,
    fc2_weight,
    fc2_bias,
    head_limit,
):
    params = (
        norm1_gain,
        norm1_bias,
        q_weight,
        q_bias,
        k_weight,
        v_weight,
        v_bias,
        o_weight,
        o_bias,
        norm2_gain,
        norm2_bias,
        fc1_weight,
        fc1_bias,
        fc2_weight,
        fc2_bias,
    )
    gathered = (
        lax.all_gather(params[0], ("dp", "seq"), axis=0, tiled=True),
        lax.all_gather(params[1], ("dp", "seq"), axis=0, tiled=True),
        lax.all_gather(params[2], ("dp", "seq"), axis=0, tiled=True),
        lax.all_gather(params[3], ("dp", "seq"), axis=0, tiled=True),
        lax.all_gather(params[4], ("dp", "seq"), axis=0, tiled=True),
        lax.all_gather(params[5], ("dp", "seq"), axis=0, tiled=True),
        lax.all_gather(params[6], ("dp", "seq"), axis=0, tiled=True),
        lax.all_gather(params[7], ("dp", "seq"), axis=0, tiled=True),
        lax.all_gather(params[8], ("dp", "seq"), axis=0, tiled=True),
        lax.all_gather(params[9], ("dp", "seq"), axis=0, tiled=True),
        lax.all_gather(params[10], ("dp", "seq"), axis=0, tiled=True),
        lax.all_gather(params[11], ("dp", "seq"), axis=0, tiled=True),
        lax.all_gather(params[12], ("dp", "seq"), axis=0, tiled=True),
        lax.all_gather(params[13], ("dp", "seq"), axis=0, tiled=True),
        lax.all_gather(params[14], ("dp", "seq"), axis=0, tiled=True),
    )
    (
        gain_one,
        shift_one,
        w_query,
        b_query,
        w_key,
        w_value,
        b_value,
        w_out,
        b_out,
        gain_two,
        shift_two,
        w_up,
        b_up,
        w_down,
        b_down,
    ) = unpack(gathered)
    seqs_dev, tokens, width = hidden_in.shape
    inputs = hidden_in.astype(jnp.float32)
    normed_one = layer_norm(inputs, gain_one, shift_one)
    low_one = normed_one.astype(jnp.bfloat16)
    queries = (project(low_one, w_query) + b_query).astype(jnp.bfloat16)
    keys = project(low_one, w_key).astype(jnp.bfloat16)
    values = (project(low_one, w_value) + b_value).astype(jnp.bfloat16)
    all_ids = lax.all_gather(block_ids, "seq", axis=1, tiled=True)
    query_pos = lax.axis_index("seq") * tokens + jnp.arange(tokens, dtype=jnp.int32)
    query_heads = queries.reshape(seqs_dev, tokens, HEADS, HEAD)
    key_heads_local = keys.reshape(seqs_dev, tokens, HEADS, HEAD)
    value_heads_local = values.reshape(seqs_dev, tokens, HEADS, HEAD)
    run_max = jnp.full((seqs_dev, HEADS, tokens), FLOOR, jnp.float32)
    peak = jnp.full((HEADS,), FLOOR, jnp.float32)
    key_part = lax.all_gather(keys, "seq", axis=1, tiled=True)
    value_part = lax.all_gather(values, "seq", axis=1, tiled=True)
    count = key_part.shape[1]
    key_heads = key_part.reshape(seqs_dev, count, HEADS, HEAD)
    value_heads = value_part.reshape(seqs_dev, count, HEADS, HEAD)
    key_ids = all_ids
    key_pos = jnp.arange(count, dtype=jnp.int32)
    raw, allowed, score = score_block(
        query_heads, key_heads, block_ids, key_ids, query_pos, key_pos
    )
    new_max = jnp.maximum(run_max, jnp.max(score, axis=-1))
    probs = jnp.exp(score - new_max[..., None])
    run_total = jnp.sum(probs, axis=-1)
    weighted = jnp.einsum(
        "shqk,skhd->sqhd",
        probs.astype(jnp.bfloat16),
        value_heads,
        preferred_element_type=jnp.float32,
    )
    peak = jnp.maximum(peak, jnp.max(jnp.where(allowed, raw, FLOOR), axis=(0, 2, 3)))
    run_max, run_total, weighted, peak = (new_max, run_total, weighted, peak)
    head_peak = lax.pmax(peak, ("dp", "seq"))
    log_total = run_max + jnp.log(run_total)
    attention = (weighted / jnp.transpose(run_total, (0, 2, 1))[..., None]).reshape(
        seqs_dev, tokens, width
    )
    attn_low = attention.astype(jnp.bfloat16)
    mixed = inputs + project(attn_low, w_out) + b_out
    normed_two = layer_norm(mixed, gain_two, shift_two)
    low_two = normed_two.astype(jnp.bfloat16)
    hidden_pre = project(low_two, w_up) + b_up
    hidden_low = activate(hidden_pre).astype(jnp.bfloat16)
    hidden_out = (mixed + project(hidden_low, w_down) + b_down).astype(jnp.bfloat16)
    regathered = (
        lax.all_gather(params[0], ("dp", "seq"), axis=0, tiled=True),
        lax.all_gather(params[1], ("dp", "seq"), axis=0, tiled=True),
        lax.all_gather(params[2], ("dp", "seq"), axis=0, tiled=True),
        lax.all_gather(params[3], ("dp", "seq"), axis=0, tiled=True),
        lax.all_gather(params[4], ("dp", "seq"), axis=0, tiled=True),
        lax.all_gather(params[5], ("dp", "seq"), axis=0, tiled=True),
        lax.all_gather(params[6], ("dp", "seq"), axis=0, tiled=True),
        lax.all_gather(params[7], ("dp", "seq"), axis=0, tiled=True),
        lax.all_gather(params[8], ("dp", "seq"), axis=0, tiled=True),
        lax.all_gather(params[9], ("dp", "seq"), axis=0, tiled=True),
        lax.all_gather(params[10], ("dp", "seq"), axis=0, tiled=True),
        lax.all_gather(params[11], ("dp", "seq"), axis=0, tiled=True),
        lax.all_gather(params[12], ("dp", "seq"), axis=0, tiled=True),
        lax.all_gather(params[13], ("dp", "seq"), axis=0, tiled=True),
        lax.all_gather(params[14], ("dp", "seq"), axis=0, tiled=True),
    )
    (
        gain_one,
        shift_one,
        w_query,
        b_query,
        w_key,
        w_value,
        b_value,
        w_out,
        b_out,
        gain_two,
        shift_two,
        w_up,
        b_up,
        w_down,
        b_down,
    ) = unpack(regathered)
    dout = out_grad.astype(jnp.float32)
    grad_b_down = jnp.sum(dout, axis=(0, 1))
    grad_w_down = rows_first(hidden_low, out_grad)
    dhidden = times_transpose(out_grad, w_down)
    _, gelu_back = jax.vjp(activate, hidden_pre)
    dpre_low = gelu_back(dhidden)[0].astype(jnp.bfloat16)
    grad_b_up = token_total(dpre_low)
    grad_w_up = rows_first(low_two, dpre_low)
    dnormed_two = times_transpose(dpre_low, w_up)
    _, norm_back_two = jax.vjp(layer_norm, mixed, gain_two, shift_two)
    dmixed_part, grad_gain_two, grad_shift_two = norm_back_two(dnormed_two)
    dmixed = dout + dmixed_part
    dbranch = dmixed.astype(jnp.bfloat16)
    grad_b_out = token_total(dbranch)
    grad_w_out = rows_first(attn_low, dbranch)
    later_terms = (
        grad_w_out,
        grad_b_out,
        grad_gain_two,
        grad_shift_two,
        grad_w_up,
        grad_b_up,
        grad_w_down,
        grad_b_down,
    )
    dattention = times_transpose(dbranch, w_out).astype(jnp.bfloat16)
    delta = jnp.transpose(
        jnp.sum(
            (dattention.astype(jnp.float32) * attention).reshape(seqs_dev, tokens, HEADS, HEAD),
            axis=-1,
        ),
        (0, 2, 1),
    )
    all_log, all_delta = (
        lax.all_gather(log_total, "seq", axis=2, tiled=True),
        lax.all_gather(delta, "seq", axis=2, tiled=True),
    )
    dout_heads = dattention.reshape(seqs_dev, tokens, HEADS, HEAD)
    key_part = lax.all_gather(keys, "seq", axis=1, tiled=True)
    value_part = lax.all_gather(values, "seq", axis=1, tiled=True)
    count = key_part.shape[1]
    key_heads = key_part.reshape(seqs_dev, count, HEADS, HEAD)
    value_heads = value_part.reshape(seqs_dev, count, HEADS, HEAD)
    key_ids = all_ids
    key_pos = jnp.arange(count, dtype=jnp.int32)
    raw, allowed, score = score_block(
        query_heads, key_heads, block_ids, key_ids, query_pos, key_pos
    )
    probs = jnp.exp(score - log_total[..., None])
    dprobs = jnp.einsum(
        "sqhd,skhd->shqk", dout_heads, value_heads, preferred_element_type=jnp.float32
    )
    dscores = (probs * (dprobs - delta[..., None])).astype(jnp.bfloat16)
    dquery = 0.125 * jnp.einsum(
        "shqk,skhd->sqhd", dscores, key_heads, preferred_element_type=jnp.float32
    )
    query_part = lax.all_gather(queries, "seq", axis=1, tiled=True)
    dout_part = lax.all_gather(dattention, "seq", axis=1, tiled=True)
    count = query_part.shape[1]
    part_queries = query_part.reshape(seqs_dev, count, HEADS, HEAD)
    part_douts = dout_part.reshape(seqs_dev, count, HEADS, HEAD)
    part_pos = jnp.arange(count, dtype=jnp.int32)
    raw, allowed, score = score_block(
        part_queries, key_heads_local, all_ids, block_ids, part_pos, query_pos
    )
    probs = jnp.exp(score - all_log[..., None])
    value_total = jnp.einsum(
        "shqk,sqhd->skhd",
        probs.astype(jnp.bfloat16),
        part_douts,
        preferred_element_type=jnp.float32,
    )
    dprobs = jnp.einsum(
        "sqhd,skhd->shqk", part_douts, value_heads_local, preferred_element_type=jnp.float32
    )
    dscores = (probs * (dprobs - all_delta[..., None])).astype(jnp.bfloat16)
    key_total = 0.125 * jnp.einsum(
        "shqk,sqhd->skhd", dscores, part_queries, preferred_element_type=jnp.float32
    )
    dquery_low = dquery.reshape(seqs_dev, tokens, width).astype(jnp.bfloat16)
    dkey_low = key_total.reshape(seqs_dev, tokens, width).astype(jnp.bfloat16)
    dvalue_low = value_total.reshape(seqs_dev, tokens, width).astype(jnp.bfloat16)
    grad_b_query = token_total(dquery_low)
    grad_b_value = token_total(dvalue_low)
    grad_w_query = rows_first(low_one, dquery_low)
    grad_w_key = rows_first(low_one, dkey_low)
    grad_w_value = rows_first(low_one, dvalue_low)
    dnormed_one = (
        times_transpose(dquery_low, w_query)
        + times_transpose(dkey_low, w_key)
        + times_transpose(dvalue_low, w_value)
    )
    _, norm_back_one = jax.vjp(layer_norm, inputs, gain_one, shift_one)
    dinputs_part, grad_gain_one, grad_shift_one = norm_back_one(dnormed_one)
    hidden_grad = (dmixed + dinputs_part).astype(jnp.bfloat16)
    earlier_terms = (
        grad_gain_one,
        grad_shift_one,
        grad_w_query,
        grad_b_query,
        grad_w_key,
        grad_w_value,
        grad_b_value,
    )
    shards = tuple(
        lax.psum_scatter(
            earlier_terms + later_terms, ("dp", "seq"), scatter_dimension=0, tiled=True
        )
    )
    factor = jnp.sqrt(head_limit / jnp.maximum(head_peak, head_limit))
    column = jnp.repeat(factor, HEAD)
    clipped_query = (q_weight.astype(jnp.float32) * column[None, :]).astype(jnp.bfloat16)
    clipped_key = (k_weight.astype(jnp.float32) * column[None, :]).astype(jnp.bfloat16)
    return (hidden_out, hidden_grad) + shards + (clipped_query, clipped_key, head_peak)


BF16 = jnp.bfloat16
F32 = jnp.float32


def lanes_dot(left, right, left_dim, right_dim):
    return lax.dot_general(
        left, right, (((left_dim,), (right_dim,)), ((), ())), preferred_element_type=F32
    )


def half_lanes(values, which):
    lane = lax.broadcasted_iota(jnp.int32, values.shape, 1)
    keep = lane < HEAD if which == 0 else lane >= HEAD
    return jnp.where(keep, values, jnp.zeros_like(values))


def attend_kernel(slopes, q_ref, k_ref, v_ref, k2_ref, v2_ref, key_ref, query_ref, out_ref, stat_ref):
    pair = pl.program_id(0)
    allowed = key_ref[:, 1:2] <= query_ref[1:2, :]
    offset = key_ref[:, 0:1] - query_ref[0:1, :]
    keys = jnp.concatenate([k_ref[...], k2_ref[...]], axis=0)
    values = jnp.concatenate([v_ref[...], v2_ref[...]], axis=0)
    queries = q_ref[...] * jnp.asarray(0.125, BF16)
    mixes, logs, peaks = [], [], []
    for a in range(2):
        raw = lanes_dot(keys, half_lanes(queries, a), 1, 1)
        score = jnp.where(allowed, raw + slopes[2 * pair + a] * offset, FLOOR)
        top = jnp.max(score, axis=0, keepdims=True)
        probs = jnp.exp(score - top)
        total = jnp.sum(probs, axis=0, keepdims=True)
        mix = lanes_dot(values, probs.astype(BF16), 0, 0)
        mixes.append(mix[a * HEAD : (a + 1) * HEAD] / total)
        logs.append(top + jnp.log(total))
        peaks.append(jnp.max(jnp.where(allowed, raw, FLOOR), axis=0, keepdims=True))
    out_ref[...] = jnp.concatenate(mixes, axis=0).T.astype(BF16)
    stat_ref[...] = jnp.concatenate(logs + peaks + logs + peaks, axis=0)


def attend_back_kernel(
    slopes, q_ref, do_ref, k_ref, v_ref, k2_ref, v2_ref, key_ref, query_ref, stat_ref,
    dq_ref, dk_ref, dv_ref,
):
    pair = pl.program_id(0)
    step = pl.program_id(1)
    allowed = key_ref[:, 1:2] <= query_ref[1:2, :]
    offset = key_ref[:, 0:1] - query_ref[0:1, :]
    keys = jnp.concatenate([k_ref[...], k2_ref[...]], axis=0)
    values = jnp.concatenate([v_ref[...], v2_ref[...]], axis=0)
    queries = q_ref[...] * jnp.asarray(0.125, BF16)
    douts = do_ref[...]
    dqs, dk, dv = [], None, None
    for a in range(2):
        query = half_lanes(queries, a)
        dout = half_lanes(douts, a)
        raw = lanes_dot(keys, query, 1, 1)
        score = jnp.where(allowed, raw + slopes[2 * pair + a] * offset, FLOOR)
        probs = jnp.exp(score - stat_ref[a : a + 1, :])
        dprobs = lanes_dot(values, dout, 1, 1)
        delta = jnp.sum(probs * dprobs, axis=0, keepdims=True)
        dscores = (probs * (dprobs - delta)).astype(BF16)
        dv_part = lanes_dot(probs.astype(BF16), dout, 1, 0)
        dk_part = lanes_dot(dscores, query, 1, 0)
        dv = dv_part if dv is None else dv + dv_part
        dk = dk_part if dk is None else dk + dk_part
        dqs.append(lanes_dot(keys, dscores, 0, 0)[a * HEAD : (a + 1) * HEAD] * 0.125)
    dq_ref[...] = jnp.concatenate(dqs, axis=0).T.astype(BF16)

    @pl.when(step == 0)
    def _():
        dk_ref[...] = dk
        dv_ref[...] = dv

    @pl.when(step > 0)
    def _():
        dk_ref[...] += dk
        dv_ref[...] += dv


def query_chunk(count):
    return 256 if count % 256 == 0 else count


def attention_specs(count, chunk, pairs):
    lanes = 2 * HEAD
    own = lambda first: pl.BlockSpec((count, lanes), lambda i, j: (0, first + i))
    return dict(
        slopes=pl.BlockSpec(memory_space=pltpu.SMEM),
        query=pl.BlockSpec((chunk, lanes), lambda i, j: (j, i)),
        key=own(pairs),
        value=own(2 * pairs),
        key_two=own(0),
        value_two=own(pairs),
        key_rows=pl.BlockSpec((2 * count, 2), lambda i, j: (0, 0)),
        query_rows=pl.BlockSpec((2, chunk), lambda i, j: (0, j)),
        stats=pl.BlockSpec((8, chunk), lambda i, j: (i, j)),
        whole=pl.BlockSpec((2 * count, lanes), lambda i, j: (0, i)),
    )


def attend(slopes, qkv, kv_two, key_rows, query_rows):
    count, pairs = qkv.shape[0], slopes.shape[0] // 2
    chunk = query_chunk(count)
    specs = attention_specs(count, chunk, pairs)
    work = 2 * count * count * 2 * HEAD * 2 * pairs
    return pl.pallas_call(
        attend_kernel,
        grid=(pairs, count // chunk),
        in_specs=[specs[n] for n in (
            "slopes", "query", "key", "value", "key_two", "value_two", "key_rows", "query_rows")],
        out_specs=[specs["query"], specs["stats"]],
        out_shape=[
            jax.ShapeDtypeStruct((count, pairs * 2 * HEAD), BF16),
            jax.ShapeDtypeStruct((pairs * 8, count), F32),
        ],
        cost_estimate=pl.CostEstimate(
            flops=4 * work, bytes_accessed=8 * count * pairs * 2 * HEAD,
            transcendentals=4 * pairs * count * count,
        ),
        compiler_params=pltpu.CompilerParams(vmem_limit_bytes=48 * 1024 * 1024),
        name="attend",
    )(slopes, qkv, qkv, qkv, kv_two, kv_two, key_rows, query_rows)


def attend_back(slopes, qkv, douts, kv_two, key_rows, query_rows, stats):
    count, pairs = qkv.shape[0], slopes.shape[0] // 2
    chunk = query_chunk(count)
    specs = attention_specs(count, chunk, pairs)
    work = 2 * count * count * 2 * HEAD * 2 * pairs
    return pl.pallas_call(
        attend_back_kernel,
        grid=(pairs, count // chunk),
        in_specs=[specs[n] for n in (
            "slopes", "query", "query", "key", "value", "key_two", "value_two", "key_rows",
            "query_rows", "stats")],
        out_specs=[specs["query"], specs["whole"], specs["whole"]],
        out_shape=[
            jax.ShapeDtypeStruct((count, pairs * 2 * HEAD), BF16),
            jax.ShapeDtypeStruct((2 * count, pairs * 2 * HEAD), F32),
            jax.ShapeDtypeStruct((2 * count, pairs * 2 * HEAD), F32),
        ],
        cost_estimate=pl.CostEstimate(
            flops=10 * work, bytes_accessed=24 * count * pairs * 2 * HEAD,
            transcendentals=4 * pairs * count * count,
        ),
        compiler_params=pltpu.CompilerParams(vmem_limit_bytes=48 * 1024 * 1024),
        name="attend_back",
    )(slopes, qkv, douts, qkv, qkv, kv_two, kv_two, key_rows, query_rows, stats)


def flips(size, step):
    return [(i, i ^ step) for i in range(size)]


def pick(values, index, axis=0):
    return lax.dynamic_index_in_dim(values, index, axis, keepdims=False)


def in_order(parts, me):
    placed = jnp.broadcast_to(parts[0][None], (len(parts),) + parts[0].shape)
    for r in range(1, len(parts)):
        placed = lax.dynamic_update_index_in_dim(placed, parts[r], me ^ r, 0)
    return placed


def split_body(planes, seq_size, *args):
    (
        hidden_in,
        block_ids,
        out_grad,
        norm1_gain,
        norm1_bias,
        q_weight,
        q_bias,
        k_weight,
        v_weight,
        v_bias,
        o_weight,
        o_bias,
        norm2_gain,
        norm2_bias,
        fc1_weight,
        fc1_bias,
        fc2_weight,
        fc2_bias,
        head_limit,
    ) = args
    chips = seq_size // 2
    plane = lax.axis_index("dp")
    spot = lax.axis_index("seq")
    chip, core = spot // 2, spot % 2
    tokens, width = hidden_in.shape[1:]
    rows = q_weight.shape[0]
    units = fc2_weight.shape[0]
    count = chips * tokens

    def to_chip(values, r):
        return lax.ppermute(values, "seq", flips(seq_size, 2 * r))

    def to_core(values):
        return lax.ppermute(values, "seq", flips(seq_size, 1))

    def to_plane(values, j):
        return lax.ppermute(values, "dp", flips(planes, j))

    def spread(values):
        parts = [values]
        for r in range(1, chips):
            parts.append(to_chip(values, r))
        return parts

    def fold(partial):
        blocks = partial.reshape(chips, tokens, width)
        total = blocks[0]
        for r in range(1, chips):
            other = to_chip(blocks[r].astype(BF16), r)
            total = total + other.astype(F32)
        return total

    def deal(parts, kind=BF16):
        dealt = [pick(parts, chip)]
        for r in range(1, chips):
            dealt.append(to_chip(pick(parts, chip ^ r).astype(kind), r))
        return dealt

    def from_planes(values):
        parts = [values]
        for j in range(1, planes):
            parts.append(to_plane(values, j))
        return in_order(parts, plane)

    def plane_total(parts, kind=BF16):
        total = pick(parts, plane)
        for j in range(1, planes):
            other = to_plane(pick(parts, plane ^ j).astype(kind), j)
            total = total + other.astype(F32)
        return total

    def weave(mine, other, axis):
        return lax.dynamic_update_index_in_dim(
            jnp.stack([mine, mine], axis=axis), other, 1 - core, axis
        )

    def column_parts(weight):
        share = weight.reshape(weight.shape[0], planes, chips, -1)
        return jnp.transpose(share, (2, 0, 1, 3)).reshape(chips, weight.shape[0], -1)

    small = jnp.concatenate(
        [
            jnp.stack(
                [
                    v.astype(F32)
                    for v in (
                        norm1_gain, norm1_bias, q_bias, v_bias,
                        o_bias, norm2_gain, norm2_bias, fc2_bias,
                    )
                ]
            ),
            fc1_bias.astype(F32).reshape(-1, rows),
            block_ids.astype(F32).reshape(-1, rows),
        ]
    )
    col_parts = jnp.concatenate(
        [column_parts(w) for w in (q_weight, k_weight, v_weight, fc1_weight)], axis=2
    )
    dealt = in_order(deal(col_parts), chip)
    table = from_planes(small)
    table = weave(table, to_core(table), 0)
    table = in_order(spread(table), chip)
    by_chip = jnp.transpose(table, (2, 0, 1, 3, 4)).reshape(planes, chips, 2, -1)
    activations = spread(jnp.concatenate([hidden_in[0], out_grad[0]], axis=0))
    hidden = jnp.concatenate([a[:tokens] for a in activations], axis=0)
    douts = jnp.concatenate([a[tokens:] for a in activations], axis=0)
    mine_by_chip = pick(by_chip, chip, 1)

    def vector(i):
        return by_chip[..., i * rows : (i + 1) * rows].reshape(width)

    def chip_vector(i):
        return mine_by_chip[..., i * rows : (i + 1) * rows].reshape(-1)

    gain_one, shift_one, b_out, gain_two, shift_two, b_down = (
        vector(i) for i in (0, 1, 4, 5, 6, 7)
    )
    b_query, b_value = chip_vector(2), chip_vector(3)
    b_up = mine_by_chip[..., 8 * rows : 8 * rows + units].reshape(-1)
    ids = pick(by_chip.reshape(planes, seq_size, -1), plane)[:, 8 * rows + units :]
    near = [spot ^ (2 * r) for r in range(chips)]
    order = near + [at ^ 1 for at in near]
    key_ids = jnp.concatenate([pick(ids, at) for at in order])
    lane = jnp.arange(tokens, dtype=jnp.int32)
    key_pos = jnp.concatenate([(at * tokens + lane).astype(F32) for at in order])
    key_rows = jnp.stack([key_pos, key_ids], axis=1)
    query_rows = jnp.stack([key_pos[:count], key_ids[:count]], axis=0)
    slope_host = 2.0 ** (-8.0 * (np.arange(HEADS, dtype=np.float64) + 1.0) / HEADS)
    slopes = pick(jnp.asarray(slope_host.reshape(planes, chips), F32), chip, 1)

    share = width // chips
    out_part = jnp.transpose(o_weight.reshape(rows, chips, share), (1, 0, 2))
    first = from_planes(jnp.concatenate([dealt[:, :, : 3 * share], out_part], axis=2))
    first_two = to_core(first)
    w_qkv = weave(first[..., : 3 * share], first_two[..., : 3 * share], 2).reshape(width, -1)
    w_out = weave(first[..., 3 * share :], first_two[..., 3 * share :], 2)
    w_out_own = jnp.transpose(w_out, (0, 2, 3, 1, 4)).reshape(share, width)
    w_out = jnp.concatenate(spread(w_out_own), axis=0)
    second = from_planes(
        jnp.concatenate([dealt[:, :, 3 * share :].reshape(chips * rows, -1), fc2_weight], axis=0),
    )
    second_two = to_core(second)
    up_mine, up_two = (
        w[:, : chips * rows].reshape(planes, chips, rows, -1) for w in (second, second_two)
    )
    w_up = weave(up_mine, up_two, 2).reshape(width, -1)
    w_down = weave(second[:, chips * rows :], second_two[:, chips * rows :], 1).reshape(-1, width)

    inputs = hidden.astype(F32)
    low_one = layer_norm(inputs, gain_one, shift_one).astype(BF16)
    qkv_bias = jnp.concatenate([b_query, jnp.zeros_like(b_query), b_value])
    qkv = (project(low_one, w_qkv) + qkv_bias).astype(BF16)
    kv_two = to_core(qkv[:, share:])
    attn_low, stats = attend(slopes, qkv, kv_two, key_rows, query_rows)
    attn_all = [part.reshape(chips, tokens, -1) for part in spread(attn_low)]
    attn_all = jnp.concatenate(
        [jnp.stack([part[j ^ r] for j in range(chips)]) for r, part in enumerate(attn_all)], axis=2
    ).reshape(count, width)
    mixed = inputs + project(attn_all, w_out) + b_out
    low_two = layer_norm(mixed, gain_two, shift_two).astype(BF16)
    hidden_pre = project(low_two, w_up) + b_up
    hidden_low, gelu_back = jax.vjp(activate, hidden_pre)
    hidden_low = hidden_low.astype(BF16)

    dhidden = times_transpose(douts, w_down)
    dpre_low = gelu_back(dhidden)[0].astype(BF16)
    dnormed_two = fold(times_transpose(dpre_low, w_up))
    mixed_own = mixed[:tokens]
    _, norm_back_two = jax.vjp(layer_norm, mixed_own, gain_two, shift_two)
    dmixed_part, grad_gain_two, grad_shift_two = norm_back_two(dnormed_two)
    dmixed = out_grad[0].astype(F32) + dmixed_part
    dbranch = jnp.concatenate(spread(dmixed.astype(BF16)), axis=0)

    def own_rows(partial):
        return partial.reshape(planes, chips, 2, rows, partial.shape[1])

    def owner_columns(parts, pieces):
        parts = in_order([p.astype(F32) for p in deal(parts)], chip)
        parts = parts.reshape(chips, rows, pieces, planes, -1)
        return jnp.transpose(parts, (2, 1, 3, 0, 4)).reshape(pieces, rows, -1)

    def core_sums(pairs, axis_out, kind=BF16):
        mine = jnp.concatenate([pick(p, core, at) for p, at in pairs], axis=axis_out)
        other = [pick(p, 1 - core, at).astype(kind) for p, at in pairs]
        return mine + to_core(jnp.concatenate(other, axis=axis_out)).astype(F32)

    ff_up = rows_first(low_two, dpre_low).reshape(planes, chips, 2, rows, -1)
    ff_up = jnp.transpose(ff_up, (0, 2, 1, 3, 4)).reshape(planes, 2, chips * rows, -1)
    ff_down = rows_first(hidden_low, douts).reshape(planes, 2, units, width)
    ff_total = plane_total(core_sums([(ff_up, 1), (ff_down, 1)], 1))
    grad_w_up = owner_columns(ff_total[: chips * rows].reshape(chips, rows, -1), 1)[0]
    grad_w_down = ff_total[chips * rows :]

    dattention = times_transpose(dbranch, w_out_own).astype(BF16)
    held_low, held_mixed, dattention = lax.optimization_barrier((hidden_low, mixed_own, dattention))
    hidden_out = (held_mixed + fold(project(held_low, w_down)) + b_down).astype(BF16)
    out_partial = rows_first(attn_low, dbranch).reshape(planes, 2, rows, chips, share)
    out_partial = jnp.transpose(out_partial, (0, 3, 1, 2, 4))
    dquery, dkey, dvalue = attend_back(slopes, qkv, dattention, kv_two, key_rows, query_rows, stats)
    dkv_two = to_core(jnp.concatenate([dkey[count:], dvalue[count:]], axis=1).astype(BF16))
    dkv = (
        jnp.concatenate([dkey[:count], dvalue[:count]], axis=1) + dkv_two.astype(F32)
    ).astype(BF16)
    dqkv = jnp.concatenate([dquery, dkv], axis=1)
    dnormed_one = fold(times_transpose(dqkv, w_qkv))
    _, norm_back_one = jax.vjp(layer_norm, inputs[:tokens], gain_one, shift_one)
    dinputs_part, grad_gain_one, grad_shift_one = norm_back_one(dnormed_one)
    hidden_grad = (dmixed + dinputs_part).astype(BF16)
    attn_total = plane_total(
        core_sums([(own_rows(rows_first(low_one, dqkv)), 2), (out_partial, 2)], 3),
    )
    grad_w_query, grad_w_key, grad_w_value = owner_columns(attn_total[..., : 3 * share], 3)
    grad_w_out = jnp.transpose(attn_total[..., 3 * share :], (1, 0, 2)).reshape(rows, width)

    norms = jnp.stack([grad_gain_one, grad_shift_one, grad_gain_two, grad_shift_two])
    norms = norms.reshape(4, planes, chips, 2, rows)
    norms = jnp.transpose(norms, (2, 1, 3, 0, 4)).reshape(chips, -1)
    peaks = jnp.max(stats.reshape(-1, 8, count)[:, 2:4], axis=2).reshape(1, planes)
    peaks = jnp.broadcast_to(jnp.pad(peaks, ((0, 0), (0, 128 - planes))), (chips, 128))
    norms = deal(jnp.concatenate([norms, peaks], axis=1), F32)
    peaks = in_order([n[-128 : planes - 128] for n in norms], chip).T.reshape(1, HEADS)
    norms = sum(n[:-128] for n in norms).reshape(planes, 2, 4 * rows)
    by_feature = jnp.stack(
        [jnp.sum(dbranch.astype(F32), axis=0), jnp.sum(douts.astype(F32), axis=0)]
    ).reshape(2, planes, chips, 2, rows)
    by_feature = jnp.transpose(pick(by_feature, chip, 2), (1, 2, 0, 3)).reshape(planes, 2, 2 * rows)
    dqkv_total = jnp.sum(dqkv.astype(F32), axis=0).reshape(3, planes, 2, rows)
    dpre_total = jnp.sum(dpre_low.astype(F32), axis=0).reshape(planes, 2, units)
    sums = jnp.concatenate([norms, dqkv_total[0], dqkv_total[2], by_feature, dpre_total], axis=2)
    peaks = jnp.pad(peaks, ((0, 0), (0, sums.shape[2] - HEADS)))
    other = to_core(jnp.concatenate([pick(sums, 1 - core, 1), peaks], axis=0))
    sums = pick(sums, core, 1) + other[:planes]
    peaks = jnp.maximum(peaks, other[planes:])[0, :128]
    total, head_peak = pick(sums, plane), peaks
    for j in range(1, planes):
        other = to_plane(jnp.concatenate([pick(sums, plane ^ j), peaks]), j)
        total = total + other[:-128]
        head_peak = jnp.maximum(head_peak, other[-128:])
    sums, head_peak = total, head_peak[:HEADS]
    (
        g_gain_one, g_shift_one, g_gain_two, g_shift_two, g_b_query, g_b_value, g_b_out, g_b_down,
    ) = (sums[i * rows : (i + 1) * rows] for i in range(8))
    g_b_up = sums[8 * rows :]

    factor = jnp.sqrt(head_limit / jnp.maximum(head_peak, head_limit))
    column = jnp.repeat(factor, HEAD)
    clipped_query = (q_weight.astype(F32) * column[None, :]).astype(BF16)
    clipped_key = (k_weight.astype(F32) * column[None, :]).astype(BF16)
    return (
        hidden_out[None],
        hidden_grad[None],
        g_gain_one,
        g_shift_one,
        grad_w_query,
        g_b_query,
        grad_w_key,
        grad_w_value,
        g_b_value,
        grad_w_out,
        g_b_out,
        g_gain_two,
        g_shift_two,
        grad_w_up,
        g_b_up,
        grad_w_down,
        g_b_down,
        clipped_query,
        clipped_key,
        head_peak,
    )


def power_of_two(number):
    return number & (number - 1) == 0


def body(planes, seq_size, *args):
    seqs_dev, _, width = args[0].shape
    chips = seq_size // 2
    heads_split = planes * chips * HEAD == width and planes % 2 == 0
    sizes_fit = seq_size % 2 == 0 and power_of_two(chips) and power_of_two(planes)
    if heads_split and sizes_fit and seqs_dev == 1:
        return split_body(planes, seq_size, *args)
    return gather_body(*args)


def solution(mesh):
    return jax.shard_map(
        functools.partial(body, mesh.shape["dp"], mesh.shape["seq"]),
        mesh=mesh,
        in_specs=(
            P("dp", "seq", None),
            P("dp", "seq"),
            P("dp", "seq", None),
            P(("dp", "seq")),
            P(("dp", "seq")),
            P(("dp", "seq"), None),
            P(("dp", "seq")),
            P(("dp", "seq"), None),
            P(("dp", "seq"), None),
            P(("dp", "seq")),
            P(("dp", "seq"), None),
            P(("dp", "seq")),
            P(("dp", "seq")),
            P(("dp", "seq")),
            P(("dp", "seq"), None),
            P(("dp", "seq")),
            P(("dp", "seq"), None),
            P(("dp", "seq")),
            P(),
        ),
        out_specs=(
            P("dp", "seq", None),
            P("dp", "seq", None),
            P(("dp", "seq")),
            P(("dp", "seq")),
            P(("dp", "seq"), None),
            P(("dp", "seq")),
            P(("dp", "seq"), None),
            P(("dp", "seq"), None),
            P(("dp", "seq")),
            P(("dp", "seq"), None),
            P(("dp", "seq")),
            P(("dp", "seq")),
            P(("dp", "seq")),
            P(("dp", "seq"), None),
            P(("dp", "seq")),
            P(("dp", "seq"), None),
            P(("dp", "seq")),
            P(("dp", "seq"), None),
            P(("dp", "seq"), None),
            P(),
        ),
        check_vma=False,
    )
```

```python
import functools
import types

import jax
import jax.numpy as jnp
import numpy as np
from jax import lax
from jax.experimental import pallas as pl
from jax.experimental.pallas import tpu as pltpu
from jax.sharding import PartitionSpec as P


BOTH = ("dp", "seq")
HEADS = 16
HEAD = 64


EPS = 1e-05
FLOOR = -1e30


def layer_norm(values, gain, shift):
    mean = jnp.mean(values, axis=-1, keepdims=True)
    centred = values - mean
    spread = jnp.mean(centred * centred, axis=-1, keepdims=True)
    return centred * lax.rsqrt(spread + EPS) * gain + shift


def activate(values):
    return jax.nn.gelu(values, approximate=True)


def slope_table():
    return 2.0 ** (-8.0 * (jnp.arange(HEADS, dtype=jnp.float32) + 1.0) / HEADS)


def score_block(query_heads, key_heads, query_ids, key_ids, query_pos, key_pos):
    raw = (
        jnp.einsum("sqhd,skhd->shqk", query_heads, key_heads, preferred_element_type=jnp.float32)
        * 0.125
    )
    allowed = (key_ids[:, None, :] <= query_ids[:, :, None])[:, None]
    offset = (key_pos[None, :] - query_pos[:, None]).astype(jnp.float32)
    score = jnp.where(allowed, raw + slope_table()[:, None, None] * offset[None], FLOOR)
    return (raw, allowed, score)


def project(values, weight):
    return jnp.dot(values, weight, preferred_element_type=jnp.float32)


def rows_first(left, right):
    flat_left = left.reshape(-1, left.shape[-1])
    flat_right = right.reshape(-1, right.shape[-1])
    return lax.dot_general(
        flat_left, flat_right, (((0,), (0,)), ((), ())), preferred_element_type=jnp.float32
    )


def times_transpose(values, weight):
    return lax.dot_general(
        values, weight, (((values.ndim - 1,), (1,)), ((), ())), preferred_element_type=jnp.float32
    )


def token_total(values):
    return jnp.sum(values.astype(jnp.float32), axis=(0, 1))


def unpack(gathered):
    (
        gain_one,
        shift_one,
        w_query,
        b_query,
        w_key,
        w_value,
        b_value,
        w_out,
        b_out,
        gain_two,
        shift_two,
        w_up,
        b_up,
        w_down,
        b_down,
    ) = gathered
    as_float = jnp.float32
    return (
        gain_one.astype(as_float),
        shift_one.astype(as_float),
        w_query,
        b_query.astype(as_float),
        w_key,
        w_value,
        b_value.astype(as_float),
        w_out,
        b_out.astype(as_float),
        gain_two.astype(as_float),
        shift_two.astype(as_float),
        w_up,
        b_up.astype(as_float),
        w_down,
        b_down.astype(as_float),
    )


def gather_body(
    hidden_in,
    block_ids,
    out_grad,
    norm1_gain,
    norm1_bias,
    q_weight,
    q_bias,
    k_weight,
    v_weight,
    v_bias,
    o_weight,
    o_bias,
    norm2_gain,
    norm2_bias,
    fc1_weight,
    fc1_bias,
    fc2_weight,
    fc2_bias,
    head_limit,
):
    params = (
        norm1_gain,
        norm1_bias,
        q_weight,
        q_bias,
        k_weight,
        v_weight,
        v_bias,
        o_weight,
        o_bias,
        norm2_gain,
        norm2_bias,
        fc1_weight,
        fc1_bias,
        fc2_weight,
        fc2_bias,
    )
    gathered = (
        lax.all_gather(params[0], BOTH, axis=0, tiled=True),
        lax.all_gather(params[1], BOTH, axis=0, tiled=True),
        lax.all_gather(params[2], BOTH, axis=0, tiled=True),
        lax.all_gather(params[3], BOTH, axis=0, tiled=True),
        lax.all_gather(params[4], BOTH, axis=0, tiled=True),
        lax.all_gather(params[5], BOTH, axis=0, tiled=True),
        lax.all_gather(params[6], BOTH, axis=0, tiled=True),
        lax.all_gather(params[7], BOTH, axis=0, tiled=True),
        lax.all_gather(params[8], BOTH, axis=0, tiled=True),
        lax.all_gather(params[9], BOTH, axis=0, tiled=True),
        lax.all_gather(params[10], BOTH, axis=0, tiled=True),
        lax.all_gather(params[11], BOTH, axis=0, tiled=True),
        lax.all_gather(params[12], BOTH, axis=0, tiled=True),
        lax.all_gather(params[13], BOTH, axis=0, tiled=True),
        lax.all_gather(params[14], BOTH, axis=0, tiled=True),
    )
    (
        gain_one,
        shift_one,
        w_query,
        b_query,
        w_key,
        w_value,
        b_value,
        w_out,
        b_out,
        gain_two,
        shift_two,
        w_up,
        b_up,
        w_down,
        b_down,
    ) = unpack(gathered)
    seqs_dev, tokens, width = hidden_in.shape
    inputs = hidden_in.astype(jnp.float32)
    normed_one = layer_norm(inputs, gain_one, shift_one)
    low_one = normed_one.astype(jnp.bfloat16)
    queries = (project(low_one, w_query) + b_query).astype(jnp.bfloat16)
    keys = project(low_one, w_key).astype(jnp.bfloat16)
    values = (project(low_one, w_value) + b_value).astype(jnp.bfloat16)
    all_ids = lax.all_gather(block_ids, "seq", axis=1, tiled=True)
    query_pos = lax.axis_index("seq") * tokens + jnp.arange(tokens, dtype=jnp.int32)
    query_heads = queries.reshape(seqs_dev, tokens, HEADS, HEAD)
    key_heads_local = keys.reshape(seqs_dev, tokens, HEADS, HEAD)
    value_heads_local = values.reshape(seqs_dev, tokens, HEADS, HEAD)
    run_max = jnp.full((seqs_dev, HEADS, tokens), FLOOR, jnp.float32)
    peak = jnp.full((HEADS,), FLOOR, jnp.float32)
    key_part = lax.all_gather(keys, "seq", axis=1, tiled=True)
    value_part = lax.all_gather(values, "seq", axis=1, tiled=True)
    count = key_part.shape[1]
    key_heads = key_part.reshape(seqs_dev, count, HEADS, HEAD)
    value_heads = value_part.reshape(seqs_dev, count, HEADS, HEAD)
    key_ids = all_ids
    key_pos = jnp.arange(count, dtype=jnp.int32)
    raw, allowed, score = score_block(
        query_heads, key_heads, block_ids, key_ids, query_pos, key_pos
    )
    new_max = jnp.maximum(run_max, jnp.max(score, axis=-1))
    probs = jnp.exp(score - new_max[..., None])
    run_total = jnp.sum(probs, axis=-1)
    weighted = jnp.einsum(
        "shqk,skhd->sqhd",
        probs.astype(jnp.bfloat16),
        value_heads,
        preferred_element_type=jnp.float32,
    )
    peak = jnp.maximum(peak, jnp.max(jnp.where(allowed, raw, FLOOR), axis=(0, 2, 3)))
    run_max, run_total, weighted, peak = (new_max, run_total, weighted, peak)
    head_peak = lax.pmax(peak, BOTH)
    log_total = run_max + jnp.log(run_total)
    attention = (weighted / jnp.transpose(run_total, (0, 2, 1))[..., None]).reshape(
        seqs_dev, tokens, width
    )
    attn_low = attention.astype(jnp.bfloat16)
    mixed = inputs + project(attn_low, w_out) + b_out
    normed_two = layer_norm(mixed, gain_two, shift_two)
    low_two = normed_two.astype(jnp.bfloat16)
    hidden_pre = project(low_two, w_up) + b_up
    hidden_low = activate(hidden_pre).astype(jnp.bfloat16)
    hidden_out = (mixed + project(hidden_low, w_down) + b_down).astype(jnp.bfloat16)
    regathered = (
        lax.all_gather(params[0], BOTH, axis=0, tiled=True),
        lax.all_gather(params[1], BOTH, axis=0, tiled=True),
        lax.all_gather(params[2], BOTH, axis=0, tiled=True),
        lax.all_gather(params[3], BOTH, axis=0, tiled=True),
        lax.all_gather(params[4], BOTH, axis=0, tiled=True),
        lax.all_gather(params[5], BOTH, axis=0, tiled=True),
        lax.all_gather(params[6], BOTH, axis=0, tiled=True),
        lax.all_gather(params[7], BOTH, axis=0, tiled=True),
        lax.all_gather(params[8], BOTH, axis=0, tiled=True),
        lax.all_gather(params[9], BOTH, axis=0, tiled=True),
        lax.all_gather(params[10], BOTH, axis=0, tiled=True),
        lax.all_gather(params[11], BOTH, axis=0, tiled=True),
        lax.all_gather(params[12], BOTH, axis=0, tiled=True),
        lax.all_gather(params[13], BOTH, axis=0, tiled=True),
        lax.all_gather(params[14], BOTH, axis=0, tiled=True),
    )
    (
        gain_one,
        shift_one,
        w_query,
        b_query,
        w_key,
        w_value,
        b_value,
        w_out,
        b_out,
        gain_two,
        shift_two,
        w_up,
        b_up,
        w_down,
        b_down,
    ) = unpack(regathered)
    dout = out_grad.astype(jnp.float32)
    grad_b_down = jnp.sum(dout, axis=(0, 1))
    grad_w_down = rows_first(hidden_low, out_grad)
    dhidden = times_transpose(out_grad, w_down)
    _, gelu_back = jax.vjp(activate, hidden_pre)
    dpre_low = gelu_back(dhidden)[0].astype(jnp.bfloat16)
    grad_b_up = token_total(dpre_low)
    grad_w_up = rows_first(low_two, dpre_low)
    dnormed_two = times_transpose(dpre_low, w_up)
    _, norm_back_two = jax.vjp(layer_norm, mixed, gain_two, shift_two)
    dmixed_part, grad_gain_two, grad_shift_two = norm_back_two(dnormed_two)
    dmixed = dout + dmixed_part
    dbranch = dmixed.astype(jnp.bfloat16)
    grad_b_out = token_total(dbranch)
    grad_w_out = rows_first(attn_low, dbranch)
    later_terms = (
        grad_w_out,
        grad_b_out,
        grad_gain_two,
        grad_shift_two,
        grad_w_up,
        grad_b_up,
        grad_w_down,
        grad_b_down,
    )
    dattention = times_transpose(dbranch, w_out).astype(jnp.bfloat16)
    delta = jnp.transpose(
        jnp.sum(
            (dattention.astype(jnp.float32) * attention).reshape(seqs_dev, tokens, HEADS, HEAD),
            axis=-1,
        ),
        (0, 2, 1),
    )
    all_log, all_delta = (
        lax.all_gather(log_total, "seq", axis=2, tiled=True),
        lax.all_gather(delta, "seq", axis=2, tiled=True),
    )
    dout_heads = dattention.reshape(seqs_dev, tokens, HEADS, HEAD)
    key_part = lax.all_gather(keys, "seq", axis=1, tiled=True)
    value_part = lax.all_gather(values, "seq", axis=1, tiled=True)
    count = key_part.shape[1]
    key_heads = key_part.reshape(seqs_dev, count, HEADS, HEAD)
    value_heads = value_part.reshape(seqs_dev, count, HEADS, HEAD)
    key_ids = all_ids
    key_pos = jnp.arange(count, dtype=jnp.int32)
    raw, allowed, score = score_block(
        query_heads, key_heads, block_ids, key_ids, query_pos, key_pos
    )
    probs = jnp.exp(score - log_total[..., None])
    dprobs = jnp.einsum(
        "sqhd,skhd->shqk", dout_heads, value_heads, preferred_element_type=jnp.float32
    )
    dscores = (probs * (dprobs - delta[..., None])).astype(jnp.bfloat16)
    dquery = 0.125 * jnp.einsum(
        "shqk,skhd->sqhd", dscores, key_heads, preferred_element_type=jnp.float32
    )
    query_part = lax.all_gather(queries, "seq", axis=1, tiled=True)
    dout_part = lax.all_gather(dattention, "seq", axis=1, tiled=True)
    count = query_part.shape[1]
    part_queries = query_part.reshape(seqs_dev, count, HEADS, HEAD)
    part_douts = dout_part.reshape(seqs_dev, count, HEADS, HEAD)
    part_pos = jnp.arange(count, dtype=jnp.int32)
    raw, allowed, score = score_block(
        part_queries, key_heads_local, all_ids, block_ids, part_pos, query_pos
    )
    probs = jnp.exp(score - all_log[..., None])
    value_total = jnp.einsum(
        "shqk,sqhd->skhd",
        probs.astype(jnp.bfloat16),
        part_douts,
        preferred_element_type=jnp.float32,
    )
    dprobs = jnp.einsum(
        "sqhd,skhd->shqk", part_douts, value_heads_local, preferred_element_type=jnp.float32
    )
    dscores = (probs * (dprobs - all_delta[..., None])).astype(jnp.bfloat16)
    key_total = 0.125 * jnp.einsum(
        "shqk,sqhd->skhd", dscores, part_queries, preferred_element_type=jnp.float32
    )
    dquery_low = dquery.reshape(seqs_dev, tokens, width).astype(jnp.bfloat16)
    dkey_low = key_total.reshape(seqs_dev, tokens, width).astype(jnp.bfloat16)
    dvalue_low = value_total.reshape(seqs_dev, tokens, width).astype(jnp.bfloat16)
    grad_b_query = token_total(dquery_low)
    grad_b_value = token_total(dvalue_low)
    grad_w_query = rows_first(low_one, dquery_low)
    grad_w_key = rows_first(low_one, dkey_low)
    grad_w_value = rows_first(low_one, dvalue_low)
    dnormed_one = (
        times_transpose(dquery_low, w_query)
        + times_transpose(dkey_low, w_key)
        + times_transpose(dvalue_low, w_value)
    )
    _, norm_back_one = jax.vjp(layer_norm, inputs, gain_one, shift_one)
    dinputs_part, grad_gain_one, grad_shift_one = norm_back_one(dnormed_one)
    hidden_grad = (dmixed + dinputs_part).astype(jnp.bfloat16)
    earlier_terms = (
        grad_gain_one,
        grad_shift_one,
        grad_w_query,
        grad_b_query,
        grad_w_key,
        grad_w_value,
        grad_b_value,
    )
    shards = tuple(
        lax.psum_scatter(
            earlier_terms + later_terms, BOTH, scatter_dimension=0, tiled=True
        )
    )
    factor = jnp.sqrt(head_limit / jnp.maximum(head_peak, head_limit))
    column = jnp.repeat(factor, HEAD)
    clipped_query = (q_weight.astype(jnp.float32) * column[None, :]).astype(jnp.bfloat16)
    clipped_key = (k_weight.astype(jnp.float32) * column[None, :]).astype(jnp.bfloat16)
    return (hidden_out, hidden_grad) + shards + (clipped_query, clipped_key, head_peak)


BF16 = jnp.bfloat16
F32 = jnp.float32


def lanes_dot(left, right, left_dim, right_dim):
    return lax.dot_general(
        left, right, (((left_dim,), (right_dim,)), ((), ())), preferred_element_type=F32
    )


def half_lanes(values, which):
    lane = lax.broadcasted_iota(jnp.int32, values.shape, 1)
    keep = lane < HEAD if which == 0 else lane >= HEAD
    return jnp.where(keep, values, jnp.zeros_like(values))


def attend_kernel(slopes, q_ref, k_ref, v_ref, k2_ref, v2_ref, key_ref, query_ref, out_ref, stat_ref):
    pair = pl.program_id(0)
    allowed = key_ref[:, 1:2] <= query_ref[1:2, :]
    offset = key_ref[:, 0:1] - query_ref[0:1, :]
    keys = jnp.concatenate([k_ref[...], k2_ref[...]], axis=0)
    values = jnp.concatenate([v_ref[...], v2_ref[...]], axis=0)
    queries = q_ref[...] * jnp.asarray(0.125, BF16)
    mixes, logs, peaks = [], [], []
    for a in range(2):
        raw = lanes_dot(keys, half_lanes(queries, a), 1, 1)
        score = jnp.where(allowed, raw + slopes[2 * pair + a] * offset, FLOOR)
        top = jnp.max(score, axis=0, keepdims=True)
        probs = jnp.exp(score - top)
        total = jnp.sum(probs, axis=0, keepdims=True)
        mix = lanes_dot(values, probs.astype(BF16), 0, 0)
        mixes.append(mix[a * HEAD : (a + 1) * HEAD] / total)
        logs.append(top + jnp.log(total))
        peaks.append(jnp.max(jnp.where(allowed, raw, FLOOR), axis=0, keepdims=True))
    out_ref[...] = jnp.concatenate(mixes, axis=0).T.astype(BF16)
    stat_ref[...] = jnp.concatenate(logs + peaks + logs + peaks, axis=0)


def attend_back_kernel(
    slopes, q_ref, do_ref, k_ref, v_ref, k2_ref, v2_ref, key_ref, query_ref, stat_ref,
    dq_ref, dk_ref, dv_ref,
):
    pair = pl.program_id(0)
    step = pl.program_id(1)
    allowed = key_ref[:, 1:2] <= query_ref[1:2, :]
    offset = key_ref[:, 0:1] - query_ref[0:1, :]
    keys = jnp.concatenate([k_ref[...], k2_ref[...]], axis=0)
    values = jnp.concatenate([v_ref[...], v2_ref[...]], axis=0)
    queries = q_ref[...] * jnp.asarray(0.125, BF16)
    douts = do_ref[...]
    dqs, dk, dv = [], None, None
    for a in range(2):
        query = half_lanes(queries, a)
        dout = half_lanes(douts, a)
        raw = lanes_dot(keys, query, 1, 1)
        score = jnp.where(allowed, raw + slopes[2 * pair + a] * offset, FLOOR)
        probs = jnp.exp(score - stat_ref[a : a + 1, :])
        dprobs = lanes_dot(values, dout, 1, 1)
        delta = jnp.sum(probs * dprobs, axis=0, keepdims=True)
        dscores = (probs * (dprobs - delta)).astype(BF16)
        dv_part = lanes_dot(probs.astype(BF16), dout, 1, 0)
        dk_part = lanes_dot(dscores, query, 1, 0)
        dv = dv_part if dv is None else dv + dv_part
        dk = dk_part if dk is None else dk + dk_part
        dqs.append(lanes_dot(keys, dscores, 0, 0)[a * HEAD : (a + 1) * HEAD] * 0.125)
    dq_ref[...] = jnp.concatenate(dqs, axis=0).T.astype(BF16)

    @pl.when(step == 0)
    def _():
        dk_ref[...] = dk
        dv_ref[...] = dv

    @pl.when(step > 0)
    def _():
        dk_ref[...] += dk
        dv_ref[...] += dv


def query_chunk(count):
    return 256 if count % 256 == 0 else count


def attention_specs(count, chunk, pairs):
    lanes = 2 * HEAD
    own = lambda first: pl.BlockSpec((count, lanes), lambda i, j: (0, first + i))
    return types.SimpleNamespace(
        slopes=pl.BlockSpec(memory_space=pltpu.SMEM),
        query=pl.BlockSpec((chunk, lanes), lambda i, j: (j, i)),
        key=own(pairs),
        value=own(2 * pairs),
        key_two=own(0),
        value_two=own(pairs),
        key_rows=pl.BlockSpec((2 * count, 2), lambda i, j: (0, 0)),
        query_rows=pl.BlockSpec((2, chunk), lambda i, j: (0, j)),
        stats=pl.BlockSpec((8, chunk), lambda i, j: (i, j)),
        whole=pl.BlockSpec((2 * count, lanes), lambda i, j: (0, i)),
    )


def attend(slopes, qkv, kv_two, key_rows, query_rows):
    count, pairs = qkv.shape[0], slopes.shape[0] // 2
    chunk = query_chunk(count)
    specs = attention_specs(count, chunk, pairs)
    work = 2 * count * count * 2 * HEAD * 2 * pairs
    return pl.pallas_call(
        attend_kernel,
        grid=(pairs, count // chunk),
        in_specs=[specs.slopes, specs.query, specs.key, specs.value, specs.key_two, specs.value_two, specs.key_rows, specs.query_rows],
        out_specs=[specs.query, specs.stats],
        out_shape=[
            jax.ShapeDtypeStruct((count, pairs * 2 * HEAD), BF16),
            jax.ShapeDtypeStruct((pairs * 8, count), F32),
        ],
        cost_estimate=pl.CostEstimate(
            flops=4 * work, bytes_accessed=8 * count * pairs * 2 * HEAD,
            transcendentals=4 * pairs * count * count,
        ),
        compiler_params=pltpu.CompilerParams(vmem_limit_bytes=48 * 1024 * 1024),
        name="attend",
    )(slopes, qkv, qkv, qkv, kv_two, kv_two, key_rows, query_rows)


def attend_back(slopes, qkv, douts, kv_two, key_rows, query_rows, stats):
    count, pairs = qkv.shape[0], slopes.shape[0] // 2
    chunk = query_chunk(count)
    specs = attention_specs(count, chunk, pairs)
    work = 2 * count * count * 2 * HEAD * 2 * pairs
    return pl.pallas_call(
        attend_back_kernel,
        grid=(pairs, count // chunk),
        in_specs=[specs.slopes, specs.query, specs.query, specs.key, specs.value, specs.key_two, specs.value_two, specs.key_rows, specs.query_rows, specs.stats],
        out_specs=[specs.query, specs.whole, specs.whole],
        out_shape=[
            jax.ShapeDtypeStruct((count, pairs * 2 * HEAD), BF16),
            jax.ShapeDtypeStruct((2 * count, pairs * 2 * HEAD), F32),
            jax.ShapeDtypeStruct((2 * count, pairs * 2 * HEAD), F32),
        ],
        cost_estimate=pl.CostEstimate(
            flops=10 * work, bytes_accessed=24 * count * pairs * 2 * HEAD,
            transcendentals=4 * pairs * count * count,
        ),
        compiler_params=pltpu.CompilerParams(vmem_limit_bytes=48 * 1024 * 1024),
        name="attend_back",
    )(slopes, qkv, douts, qkv, qkv, kv_two, kv_two, key_rows, query_rows, stats)


def flips(size, step):
    return [(i, i ^ step) for i in range(size)]


def pick(values, index, axis=0):
    return lax.dynamic_index_in_dim(values, index, axis, keepdims=False)


def in_order(parts, me):
    placed = jnp.broadcast_to(parts[0][None], (len(parts),) + parts[0].shape)
    for r in range(1, len(parts)):
        placed = lax.dynamic_update_index_in_dim(placed, parts[r], me ^ r, 0)
    return placed


def split_body(planes, seq_size, *args):
    (
        hidden_in,
        block_ids,
        out_grad,
        norm1_gain,
        norm1_bias,
        q_weight,
        q_bias,
        k_weight,
        v_weight,
        v_bias,
        o_weight,
        o_bias,
        norm2_gain,
        norm2_bias,
        fc1_weight,
        fc1_bias,
        fc2_weight,
        fc2_bias,
        head_limit,
    ) = args
    chips = seq_size // 2
    plane = lax.axis_index("dp")
    spot = lax.axis_index("seq")
    chip, core = spot // 2, spot % 2
    tokens, width = hidden_in.shape[1:]
    rows = q_weight.shape[0]
    units = fc2_weight.shape[0]
    count = chips * tokens

    def to_chip(values, r):
        return lax.ppermute(values, "seq", flips(seq_size, 2 * r))

    def to_core(values):
        return lax.ppermute(values, "seq", flips(seq_size, 1))

    def to_plane(values, j):
        return lax.ppermute(values, "dp", flips(planes, j))

    def spread(values):
        parts = [values]
        for r in range(1, chips):
            parts.append(to_chip(values, r))
        return parts

    def fold(partial):
        blocks = partial.reshape(chips, tokens, width)
        total = blocks[0]
        for r in range(1, chips):
            other = to_chip(blocks[r].astype(BF16), r)
            total = total + other.astype(F32)
        return total

    def deal(parts, kind=BF16):
        dealt = [pick(parts, chip)]
        for r in range(1, chips):
            dealt.append(to_chip(pick(parts, chip ^ r).astype(kind), r))
        return dealt

    def from_planes(values):
        parts = [values]
        for j in range(1, planes):
            parts.append(to_plane(values, j))
        return in_order(parts, plane)

    def plane_total(parts, kind=BF16):
        total = pick(parts, plane)
        for j in range(1, planes):
            other = to_plane(pick(parts, plane ^ j).astype(kind), j)
            total = total + other.astype(F32)
        return total

    def weave(mine, other, axis):
        return lax.dynamic_update_index_in_dim(
            jnp.stack([mine, mine], axis=axis), other, 1 - core, axis
        )

    def column_parts(weight):
        share = weight.reshape(weight.shape[0], planes, chips, -1)
        return jnp.transpose(share, (2, 0, 1, 3)).reshape(chips, weight.shape[0], -1)

    small = jnp.concatenate(
        [
            jnp.stack(
                [
                    v.astype(F32)
                    for v in (
                        norm1_gain, norm1_bias, q_bias, v_bias,
                        o_bias, norm2_gain, norm2_bias, fc2_bias,
                    )
                ]
            ),
            fc1_bias.astype(F32).reshape(-1, rows),
            block_ids.astype(F32).reshape(-1, rows),
        ]
    )
    col_parts = jnp.concatenate(
        [column_parts(w) for w in (q_weight, k_weight, v_weight, fc1_weight)], axis=2
    )
    dealt = in_order(deal(col_parts), chip)
    table = from_planes(small)
    table = weave(table, to_core(table), 0)
    table = in_order(spread(table), chip)
    by_chip = jnp.transpose(table, (2, 0, 1, 3, 4)).reshape(planes, chips, 2, -1)
    activations = spread(jnp.concatenate([hidden_in[0], out_grad[0]], axis=0))
    hidden = jnp.concatenate([a[:tokens] for a in activations], axis=0)
    douts = jnp.concatenate([a[tokens:] for a in activations], axis=0)
    mine_by_chip = pick(by_chip, chip, 1)

    def vector(i):
        return by_chip[..., i * rows : (i + 1) * rows].reshape(width)

    def chip_vector(i):
        return mine_by_chip[..., i * rows : (i + 1) * rows].reshape(-1)

    gain_one, shift_one, b_out, gain_two, shift_two, b_down = (
        vector(i) for i in (0, 1, 4, 5, 6, 7)
    )
    b_query, b_value = chip_vector(2), chip_vector(3)
    b_up = mine_by_chip[..., 8 * rows : 8 * rows + units].reshape(-1)
    ids = pick(by_chip.reshape(planes, seq_size, -1), plane)[:, 8 * rows + units :]
    near = [spot ^ (2 * r) for r in range(chips)]
    order = near + [at ^ 1 for at in near]
    key_ids = jnp.concatenate([pick(ids, at) for at in order])
    lane = jnp.arange(tokens, dtype=jnp.int32)
    key_pos = jnp.concatenate([(at * tokens + lane).astype(F32) for at in order])
    key_rows = jnp.stack([key_pos, key_ids], axis=1)
    query_rows = jnp.stack([key_pos[:count], key_ids[:count]], axis=0)
    slope_host = 2.0 ** (-8.0 * (np.arange(HEADS, dtype=np.float64) + 1.0) / HEADS)
    slopes = pick(jnp.asarray(slope_host.reshape(planes, chips), F32), chip, 1)

    share = width // chips
    out_part = jnp.transpose(o_weight.reshape(rows, chips, share), (1, 0, 2))
    first = from_planes(jnp.concatenate([dealt[:, :, : 3 * share], out_part], axis=2))
    first_two = to_core(first)
    w_qkv = weave(first[..., : 3 * share], first_two[..., : 3 * share], 2).reshape(width, -1)
    w_out = weave(first[..., 3 * share :], first_two[..., 3 * share :], 2)
    w_out_own = jnp.transpose(w_out, (0, 2, 3, 1, 4)).reshape(share, width)
    w_out = jnp.concatenate(spread(w_out_own), axis=0)
    second = from_planes(
        jnp.concatenate([dealt[:, :, 3 * share :].reshape(chips * rows, -1), fc2_weight], axis=0),
    )
    second_two = to_core(second)
    up_mine, up_two = (
        w[:, : chips * rows].reshape(planes, chips, rows, -1) for w in (second, second_two)
    )
    w_up = weave(up_mine, up_two, 2).reshape(width, -1)
    w_down = weave(second[:, chips * rows :], second_two[:, chips * rows :], 1).reshape(-1, width)

    inputs = hidden.astype(F32)
    low_one = layer_norm(inputs, gain_one, shift_one).astype(BF16)
    qkv_bias = jnp.concatenate([b_query, jnp.zeros_like(b_query), b_value])
    qkv = (project(low_one, w_qkv) + qkv_bias).astype(BF16)
    kv_two = to_core(qkv[:, share:])
    attn_low, stats = attend(slopes, qkv, kv_two, key_rows, query_rows)
    attn_all = [part.reshape(chips, tokens, -1) for part in spread(attn_low)]
    attn_all = jnp.concatenate(
        [jnp.stack([part[j ^ r] for j in range(chips)]) for r, part in enumerate(attn_all)], axis=2
    ).reshape(count, width)
    mixed = inputs + project(attn_all, w_out) + b_out
    low_two = layer_norm(mixed, gain_two, shift_two).astype(BF16)
    hidden_pre = project(low_two, w_up) + b_up
    hidden_low, gelu_back = jax.vjp(activate, hidden_pre)
    hidden_low = hidden_low.astype(BF16)

    dhidden = times_transpose(douts, w_down)
    dpre_low = gelu_back(dhidden)[0].astype(BF16)
    dnormed_two = fold(times_transpose(dpre_low, w_up))
    mixed_own = mixed[:tokens]
    _, norm_back_two = jax.vjp(layer_norm, mixed_own, gain_two, shift_two)
    dmixed_part, grad_gain_two, grad_shift_two = norm_back_two(dnormed_two)
    dmixed = out_grad[0].astype(F32) + dmixed_part
    dbranch = jnp.concatenate(spread(dmixed.astype(BF16)), axis=0)

    def own_rows(partial):
        return partial.reshape(planes, chips, 2, rows, partial.shape[1])

    def owner_columns(parts, pieces):
        parts = in_order([p.astype(F32) for p in deal(parts)], chip)
        parts = parts.reshape(chips, rows, pieces, planes, -1)
        return jnp.transpose(parts, (2, 1, 3, 0, 4)).reshape(pieces, rows, -1)

    def core_sums(pairs, axis_out, kind=BF16):
        mine = jnp.concatenate([pick(p, core, at) for p, at in pairs], axis=axis_out)
        other = [pick(p, 1 - core, at).astype(kind) for p, at in pairs]
        return mine + to_core(jnp.concatenate(other, axis=axis_out)).astype(F32)

    ff_up = rows_first(low_two, dpre_low).reshape(planes, chips, 2, rows, -1)
    ff_up = jnp.transpose(ff_up, (0, 2, 1, 3, 4)).reshape(planes, 2, chips * rows, -1)
    ff_down = rows_first(hidden_low, douts).reshape(planes, 2, units, width)
    ff_total = plane_total(core_sums([(ff_up, 1), (ff_down, 1)], 1))
    grad_w_up = owner_columns(ff_total[: chips * rows].reshape(chips, rows, -1), 1)[0]
    grad_w_down = ff_total[chips * rows :]

    dattention = times_transpose(dbranch, w_out_own).astype(BF16)
    held_low, held_mixed, dattention = lax.optimization_barrier((hidden_low, mixed_own, dattention))
    hidden_out = (held_mixed + fold(project(held_low, w_down)) + b_down).astype(BF16)
    out_partial = rows_first(attn_low, dbranch).reshape(planes, 2, rows, chips, share)
    out_partial = jnp.transpose(out_partial, (0, 3, 1, 2, 4))
    dquery, dkey, dvalue = attend_back(slopes, qkv, dattention, kv_two, key_rows, query_rows, stats)
    dkv_two = to_core(jnp.concatenate([dkey[count:], dvalue[count:]], axis=1).astype(BF16))
    dkv = (
        jnp.concatenate([dkey[:count], dvalue[:count]], axis=1) + dkv_two.astype(F32)
    ).astype(BF16)
    dqkv = jnp.concatenate([dquery, dkv], axis=1)
    dnormed_one = fold(times_transpose(dqkv, w_qkv))
    _, norm_back_one = jax.vjp(layer_norm, inputs[:tokens], gain_one, shift_one)
    dinputs_part, grad_gain_one, grad_shift_one = norm_back_one(dnormed_one)
    hidden_grad = (dmixed + dinputs_part).astype(BF16)
    attn_total = plane_total(
        core_sums([(own_rows(rows_first(low_one, dqkv)), 2), (out_partial, 2)], 3),
    )
    grad_w_query, grad_w_key, grad_w_value = owner_columns(attn_total[..., : 3 * share], 3)
    grad_w_out = jnp.transpose(attn_total[..., 3 * share :], (1, 0, 2)).reshape(rows, width)

    norms = jnp.stack([grad_gain_one, grad_shift_one, grad_gain_two, grad_shift_two])
    norms = norms.reshape(4, planes, chips, 2, rows)
    norms = jnp.transpose(norms, (2, 1, 3, 0, 4)).reshape(chips, -1)
    peaks = jnp.max(stats.reshape(-1, 8, count)[:, 2:4], axis=2).reshape(1, planes)
    peaks = jnp.broadcast_to(jnp.pad(peaks, ((0, 0), (0, 128 - planes))), (chips, 128))
    norms = deal(jnp.concatenate([norms, peaks], axis=1), F32)
    peaks = in_order([n[-128 : planes - 128] for n in norms], chip).T.reshape(1, HEADS)
    norms = sum(n[:-128] for n in norms).reshape(planes, 2, 4 * rows)
    by_feature = jnp.stack(
        [jnp.sum(dbranch.astype(F32), axis=0), jnp.sum(douts.astype(F32), axis=0)]
    ).reshape(2, planes, chips, 2, rows)
    by_feature = jnp.transpose(pick(by_feature, chip, 2), (1, 2, 0, 3)).reshape(planes, 2, 2 * rows)
    dqkv_total = jnp.sum(dqkv.astype(F32), axis=0).reshape(3, planes, 2, rows)
    dpre_total = jnp.sum(dpre_low.astype(F32), axis=0).reshape(planes, 2, units)
    sums = jnp.concatenate([norms, dqkv_total[0], dqkv_total[2], by_feature, dpre_total], axis=2)
    peaks = jnp.pad(peaks, ((0, 0), (0, sums.shape[2] - HEADS)))
    other = to_core(jnp.concatenate([pick(sums, 1 - core, 1), peaks], axis=0))
    sums = pick(sums, core, 1) + other[:planes]
    peaks = jnp.maximum(peaks, other[planes:])[0, :128]
    total, head_peak = pick(sums, plane), peaks
    for j in range(1, planes):
        other = to_plane(jnp.concatenate([pick(sums, plane ^ j), peaks]), j)
        total = total + other[:-128]
        head_peak = jnp.maximum(head_peak, other[-128:])
    sums, head_peak = total, head_peak[:HEADS]
    (
        g_gain_one, g_shift_one, g_gain_two, g_shift_two, g_b_query, g_b_value, g_b_out, g_b_down,
    ) = (sums[i * rows : (i + 1) * rows] for i in range(8))
    g_b_up = sums[8 * rows :]

    factor = jnp.sqrt(head_limit / jnp.maximum(head_peak, head_limit))
    column = jnp.repeat(factor, HEAD)
    clipped_query = (q_weight.astype(F32) * column[None, :]).astype(BF16)
    clipped_key = (k_weight.astype(F32) * column[None, :]).astype(BF16)
    return (
        hidden_out[None],
        hidden_grad[None],
        g_gain_one,
        g_shift_one,
        grad_w_query,
        g_b_query,
        grad_w_key,
        grad_w_value,
        g_b_value,
        grad_w_out,
        g_b_out,
        g_gain_two,
        g_shift_two,
        grad_w_up,
        g_b_up,
        grad_w_down,
        g_b_down,
        clipped_query,
        clipped_key,
        head_peak,
    )


def power_of_two(number):
    return number & (number - 1) == 0


def body(planes, seq_size, *args):
    seqs_dev, _, width = args[0].shape
    chips = seq_size // 2
    heads_split = planes * chips * HEAD == width and planes % 2 == 0
    sizes_fit = seq_size % 2 == 0 and power_of_two(chips) and power_of_two(planes)
    if heads_split and sizes_fit and seqs_dev == 1:
        return split_body(planes, seq_size, *args)
    return gather_body(*args)


def solution(mesh):
    return jax.shard_map(
        functools.partial(body, mesh.shape["dp"], mesh.shape["seq"]),
        mesh=mesh,
        in_specs=(
            P("dp", "seq", None),
            P(*BOTH),
            P("dp", "seq", None),
            P(BOTH),
            P(BOTH),
            P(BOTH, None),
            P(BOTH),
            P(BOTH, None),
            P(BOTH, None),
            P(BOTH),
            P(BOTH, None),
            P(BOTH),
            P(BOTH),
            P(BOTH),
            P(BOTH, None),
            P(BOTH),
            P(BOTH, None),
            P(BOTH),
            P(),
        ),
        out_specs=(
            P("dp", "seq", None),
            P("dp", "seq", None),
            P(BOTH),
            P(BOTH),
            P(BOTH, None),
            P(BOTH),
            P(BOTH, None),
            P(BOTH, None),
            P(BOTH),
            P(BOTH, None),
            P(BOTH),
            P(BOTH),
            P(BOTH),
            P(BOTH, None),
            P(BOTH),
            P(BOTH, None),
            P(BOTH),
            P(BOTH, None),
            P(BOTH, None),
            P(),
        ),
        check_vma=False,
    )
```
